512 devices in a mesh: ep: 128 (over y_lo, x, z), dp: 4 (over y_hi, core).
Axes of the slice: x: 4, y: 4 (y_hi: 2, y_lo: 2; y = y_hi * 2 + y_lo), z: 16, core: 2. Of those that a mesh axis runs over, the one named last changes fastest.
Arguments:
- tokens: bfloat16 [32768, 2048], P(('dp', 'ep')), parts along dimension 0, may hold values from -6 to 6
- gates: float32 [32768, 8], P(('dp', 'ep')), parts along dimension 0, may hold values from 0.05 to 1
- expert_ids: int32 [32768, 8], P(('dp', 'ep')), parts along dimension 0, may hold values from 0 to 31, all different within a row; in each aligned block of 64 rows (0 to 63, 64 to 127, ...) at most 20 rows name the same one
- slot_expert: int32 [128], P('dp'), parts along dimension 0, may hold values from 0 to 31, each once
- w_in: bfloat16 [512, 2, 192, 2048], P(('dp', 'ep')), parts along dimension 0, may hold values from -0.125 to 0.125
- w_out: bfloat16 [512, 192, 2048], P(('dp', 'ep')), parts along dimension 0, may hold values from -0.21875 to 0.21875
Outputs:
- mixed: bfloat16 [32768, 2048], P(('dp', 'ep')), parts along dimension 0
The draws below stay inside these ranges and needn't reach their ends.
There are 4 independent parts, one for each index of `dp`. The reference program is written for one: setup_inputs(seed, part) draws one part's arguments, and reference() takes and returns one part's arrays. A program takes and returns all parts, laid end to end along the dimension named above; each array names one. Nothing has to cross between parts.
All inputs are finite; a program needn't handle non-finite values.
Results may differ from the reference program's by a relative error of at most 0.0058.
Values may be sent and summed in bfloat16 or wider, within the bound.
A program may use at most 64 MiB of HBM per device.

```python
import math
import jax
import jax.numpy as jnp
import numpy as np
from jax import lax

D = 2048
FF = 768
GROUP = 4
TOK_DEV = 64
FF_DEV = 192
EXPERTS = 32
TOP = 8
TOKENS = 8192
CAPE = 20
N_EP = 128


def block_levels(rng, dims, shards, smallest, largest):
    gain = 1.0
    for dim, shards_of in shards:
        steps = jax.random.uniform(jax.random.fold_in(jax.random.fold_in(rng, 6), dim), (shards_of,), jnp.float32, smallest / len(shards), largest / len(shards))
        gain = gain * jnp.repeat(jnp.exp(steps), dims[dim] // shards_of).reshape((-1,) + (1,) * (len(dims) - 1 - dim))
    return gain


def routed_block(stream_key, own, number, rows, number_of, top, most, lean):
    ranking = jax.random.permutation(stream_key, number_of)
    heavy_load, ordinary = portions_of(number_of, rows * top, most, lean, True), portions_of(number_of, rows * top, most, lean, False)
    places = jnp.arange(number_of)

    def named(lengths, rotation):
        used = int((lengths > 0).sum())
        fixed = max(1, used // 4)
        shifted = fixed + (places - fixed + rotation * (used - fixed)) % max(1, number_of - fixed)
        return jnp.zeros((number_of,), jnp.int32).at[ranking[jnp.where(places < fixed, places, shifted)]].set(jnp.asarray(lengths, jnp.int32))

    lengths = jnp.where(number % 4 == 0, named(heavy_load, number // 4), named(ordinary, number - number // 4 - 1))
    mixed = jax.random.permutation(jax.random.fold_in(own, 3), number_of)
    source_of, sink = mixed[0:number_of // 2 * 2:2], mixed[1:number_of // 2 * 2:2]
    margin = jnp.minimum(lengths[source_of] - 1, most - lengths[sink]) // 2
    margin = jnp.where((source_of == ranking[0]) | (sink == ranking[0]) | (lengths[sink] == 0), 0, jnp.maximum(margin, 0))
    shifted = jax.random.randint(jax.random.fold_in(own, 4), (number_of // 2,), 0, 1 << 20) % (margin + 1)
    lengths = lengths.at[source_of].add(-shifted).at[sink].add(shifted)
    items = jnp.searchsorted(jnp.cumsum(lengths), jnp.arange(rows * top), side="right").astype(jnp.int32)
    table = items.reshape(top, rows).T
    table = table[jax.random.permutation(jax.random.fold_in(own, 1), rows)]
    rotation = jax.random.randint(jax.random.fold_in(own, 2), (rows, 1), 0, top)
    return jnp.take_along_axis(table, (jnp.arange(top)[None, :] + rotation) % top, axis=1)


def portions_of(count, total, most, lean, full):
    weights = [(1 << 20) // math.isqrt(standing ** lean) + 1 for standing in range(1, count + 1)]
    largest = most if full else min(most, max(-(-total // count), total * weights[0] // sum(weights)))
    least = 1 if total - largest >= count - 1 else 0
    holding, spare = [largest] + [least] * (count - 1), total - largest - least * (count - 1)
    while spare > 0:
        free = [i for i in range(1, count) if holding[i] < largest] or [i for i in range(1, count) if holding[i] < most]
        pool, budget = sum([weights[i] for i in free]), spare
        for i in free:
            more = min(most - holding[i], max(1, budget * weights[i] // pool), spare)
            holding[i] = holding[i] + more
            spare = spare - more
    return np.array(holding)


def bell_draw(rng, dims, scale, most, pieces=(), kind=jnp.bfloat16):
    values = scale * jax.random.normal(rng, dims, jnp.float32)
    if pieces:
        values = values * block_levels(rng, dims, pieces, -0.22, 0.18)
    return jnp.clip(values, -most, most).astype(kind)


def setup_inputs(seed: int = 0, part: int = 0) -> dict:
    keys = jax.random.split(jax.random.key(seed), 7)
    part_keys = jax.random.split(jax.random.fold_in(keys[6], part), 7)
    tokens = bell_draw(part_keys[0], (TOKENS, D), 1.0, 6.0, ((0, 128),))
    gates = jnp.clip(jnp.exp(math.log(1.0) - 2.9957323 * jax.random.uniform(part_keys[1], (TOKENS, TOP), jnp.float32) ** block_levels(part_keys[1], (TOKENS, TOP), ((0, 128),), -0.2, 0.2)), 0.05, 1.0)
    expert_ids_keys = jax.random.split(jax.random.fold_in(part_keys[2], 1), TOKENS // TOK_DEV)
    expert_ids_turns = jax.random.permutation(jax.random.fold_in(part_keys[2], 3), TOKENS // TOK_DEV)
    expert_ids = jax.vmap(lambda own, number: routed_block(jax.random.fold_in(part_keys[2], 2), own, number, TOK_DEV, EXPERTS, TOP, CAPE, 2))(expert_ids_keys, expert_ids_turns).reshape((TOKENS, TOP))
    slot_expert = jax.random.permutation(part_keys[3], EXPERTS).astype(jnp.int32)
    w_in = bell_draw(part_keys[4], (N_EP, 2, FF_DEV, D), D ** -0.5, 0.125, ((0, 128),))
    w_out = bell_draw(part_keys[5], (N_EP, FF_DEV, D), FF ** -0.5, 0.21875, ((0, 128),))
    return {"tokens": tokens, "gates": gates, "expert_ids": expert_ids, "slot_expert": slot_expert, "w_in": w_in, "w_out": w_out}


def reference(tokens, gates, expert_ids, slot_expert, w_in, w_out):
    expert_range = jnp.arange(EXPERTS, dtype=jnp.int32)
    home = jnp.zeros((EXPERTS,), jnp.int32).at[slot_expert].set(expert_range)
    flat_ids = expert_ids.reshape(-1)
    order = jnp.argsort(flat_ids, stable=True).astype(jnp.int32)
    counts = jnp.sum((flat_ids[:, None] == expert_range[None, :]).astype(jnp.int32), axis=0)
    starts = (jnp.cumsum(counts) - counts).astype(jnp.int32)
    limit = N_EP * CAPE
    padded = jnp.concatenate([order, jnp.zeros((limit,), jnp.int32)])
    gate_flat = gates.reshape(-1)

    def visit(total, expert):
        index_rows = lax.dynamic_slice(padded, (starts[expert].astype(jnp.int32),), (limit,))
        valid = jnp.arange(limit, dtype=jnp.int32) < counts[expert]
        source_token = index_rows // TOP
        chosen = tokens[source_token].astype(jnp.float32)
        first = (home[expert] * GROUP).astype(jnp.int32)
        weights_in = lax.dynamic_slice_in_dim(w_in, first, GROUP, 0).astype(jnp.float32)
        weights_out = lax.dynamic_slice_in_dim(w_out, first, GROUP, 0).astype(jnp.float32)
        gate_part = jnp.einsum("rd,jfd->rjf", chosen, weights_in[:, 0])
        up_part = jnp.einsum("rd,jfd->rjf", chosen, weights_in[:, 1])
        hidden = (jax.nn.silu(gate_part) * up_part).astype(jnp.bfloat16)
        result = jnp.einsum("rjf,jfd->rd", hidden.astype(jnp.float32), weights_out).astype(jnp.bfloat16)
        weight = jnp.where(valid, gate_flat[index_rows], jnp.zeros((), gate_flat.dtype))
        total = total.at[source_token].add(weight[:, None].astype(jnp.float32) * result.astype(jnp.float32))
        return total, None

    total, unused = lax.scan(visit, jnp.zeros((TOKENS, D), jnp.float32), expert_range)
    return total.astype(jnp.bfloat16)
```

```python
import functools

import jax
import jax.numpy as jnp
from jax import lax
from jax.experimental import pallas as pl
from jax.experimental.pallas import tpu as pltpu
from jax.sharding import PartitionSpec as P

MESH = pl.DeviceIdType.MESH
GROUP = 4
CAPE = 20
Z = 16
X = 4
Y = 2
RING = Z // 2
COLS = X * Y


def z_place():
    me = lax.axis_index("ep")
    z = me % Z
    return me - z, z


def neighbours():
    base, z = z_place()
    return base + (z + 2) % Z, base + (z + Z - 2) % Z


def signal_all(devices):
    barrier = pltpu.get_barrier_semaphore()
    for device in devices:
        pl.semaphore_signal(barrier, inc=1, device_id={"ep": device}, device_id_type=MESH)
    pl.semaphore_wait(barrier, len(devices))


def gather_kernel(tok_ref, meta_ref, out_ref, mout_ref, local_sem, send_sem, recv_sem):
    base, z = z_place()
    m = z // 2
    ends = neighbours()
    half = tok_ref.shape[0] // 2
    signal_all(ends)
    own = pltpu.make_async_copy(tok_ref, out_ref.at[m], local_sem.at[0])
    own_meta = pltpu.make_async_copy(meta_ref, mout_ref.at[m], local_sem.at[1])
    own.start()
    own_meta.start()

    def copy(way, step, chunk):
        owner = (m + (RING - step if way == 0 else step)) % RING
        if chunk == 2:
            src = meta_ref if step == 0 else mout_ref.at[owner]
            dst = mout_ref.at[owner]
        else:
            rows = pl.ds(chunk * half, half)
            src = tok_ref.at[rows] if step == 0 else out_ref.at[owner, rows]
            dst = out_ref.at[owner, rows]
        return pltpu.make_async_remote_copy(
            src_ref=src,
            dst_ref=dst,
            send_sem=send_sem.at[way, step, chunk],
            recv_sem=recv_sem.at[way, step, chunk],
            device_id={"ep": ends[way]},
            device_id_type=MESH,
        )

    last = RING // 2 - 1
    started, unread = [], {}
    for step in range(last + 1):
        for chunk in (2, 0, 1):
            for way in (0, 1):
                if step == last and way != (0 if chunk in (0, 2) else 1):
                    continue
                if step > 0:
                    unread.pop((way, step - 1, chunk)).wait_recv()
                sent = copy(way, step, chunk)
                sent.start()
                started.append(sent)
                unread[way, step, chunk] = sent
    for sent in unread.values():
        sent.wait_recv()
    for sent in started:
        sent.wait_send()
    own.wait()
    own_meta.wait()


def z_gather(tokens, meta):
    rows, width = tokens.shape
    return pl.pallas_call(
        gather_kernel,
        out_shape=(
            jax.ShapeDtypeStruct((RING, rows, width), tokens.dtype),
            jax.ShapeDtypeStruct((RING,) + meta.shape, meta.dtype),
        ),
        in_specs=[pl.BlockSpec(memory_space=pl.ANY)] * 2,
        out_specs=[pl.BlockSpec(memory_space=pl.ANY)] * 2,
        scratch_shapes=[
            pltpu.SemaphoreType.DMA((2,)),
            pltpu.SemaphoreType.DMA((2, RING // 2, 3)),
            pltpu.SemaphoreType.DMA((2, RING // 2, 3)),
        ],
        compiler_params=pltpu.CompilerParams(collective_id=0, has_side_effects=True),
        name="z_gather",
    )(tokens, meta)


def columns():
    me = lax.axis_index("ep")
    y, x, z = me // (X * Z), me // Z % X, me % Z
    others = []
    for ky in range(Y):
        for kx in range(X):
            if kx or ky:
                others.append(((y + ky) % Y) * X + (x + kx) % X)
    return y * X + x, z, others


def exchange(send_ref, recv_ref, local_sem, send_sem, recv_sem):
    mine, z, others = columns()
    own = pltpu.make_async_copy(send_ref.at[mine], recv_ref.at[mine], local_sem.at[0])
    own.start()
    copies = []
    for k, other in enumerate(others):
        copies.append(
            pltpu.make_async_remote_copy(
                src_ref=send_ref.at[other],
                dst_ref=recv_ref.at[mine],
                send_sem=send_sem.at[k],
                recv_sem=recv_sem.at[k],
                device_id={"ep": other * Z + z},
                device_id_type=MESH,
            )
        )
    for sent in copies:
        sent.start()
    return own, copies


def out_kernel(
    send_ref, win_ref, wout_ref, recv_ref, win2_ref, wout2_ref,
    local_sem, send_sem, recv_sem, wlocal_sem, wsend_sem, wrecv_sem,
):
    mine, z, others = columns()
    member = z % 2
    partner = mine * Z + z + 1 - 2 * member
    signal_all([other * Z + z for other in others] + [partner])
    own, copies = exchange(send_ref, recv_ref, local_sem, send_sem, recv_sem)
    pieces = [
        (win_ref.at[0, 0], win2_ref.at[0, member]),
        (win_ref.at[0, 1], win2_ref.at[1, member]),
        (wout_ref.at[0], wout2_ref.at[member]),
    ]
    kept = []
    for k, (src, dst) in enumerate(pieces):
        copies.append(
            pltpu.make_async_remote_copy(
                src_ref=src,
                dst_ref=dst,
                send_sem=wsend_sem.at[k],
                recv_sem=wrecv_sem.at[k],
                device_id={"ep": partner},
                device_id_type=MESH,
            )
        )
        copies[-1].start()
        kept.append(pltpu.make_async_copy(src, dst, wlocal_sem.at[k]))
        kept[-1].start()
    for sent in copies:
        sent.wait()
    own.wait()
    for piece in kept:
        piece.wait()


def xy_out(send, w_in, w_out):
    _, two, ff, width = w_in.shape
    return pl.pallas_call(
        out_kernel,
        out_shape=(
            jax.ShapeDtypeStruct(send.shape, send.dtype),
            jax.ShapeDtypeStruct((two, 2, ff, width), w_in.dtype),
            jax.ShapeDtypeStruct((2, ff, width), w_out.dtype),
        ),
        in_specs=[pl.BlockSpec(memory_space=pl.ANY)] * 3,
        out_specs=[pl.BlockSpec(memory_space=pl.ANY)] * 3,
        scratch_shapes=[
            pltpu.SemaphoreType.DMA((1,)),
            pltpu.SemaphoreType.DMA((COLS - 1,)),
            pltpu.SemaphoreType.DMA((COLS - 1,)),
            pltpu.SemaphoreType.DMA((3,)),
            pltpu.SemaphoreType.DMA((3,)),
            pltpu.SemaphoreType.DMA((3,)),
        ],
        compiler_params=pltpu.CompilerParams(collective_id=1, has_side_effects=True),
        name="xy_out",
    )(send, w_in, w_out)


def back_kernel(send_ref, recv_ref, local_sem, send_sem, recv_sem):
    mine, z, others = columns()
    signal_all([other * Z + z for other in others])
    own, copies = exchange(send_ref, recv_ref, local_sem, send_sem, recv_sem)
    for sent in copies:
        sent.wait()
    own.wait()


def xy_back(send):
    return pl.pallas_call(
        back_kernel,
        out_shape=jax.ShapeDtypeStruct(send.shape, send.dtype),
        in_specs=[pl.BlockSpec(memory_space=pl.ANY)],
        out_specs=pl.BlockSpec(memory_space=pl.ANY),
        scratch_shapes=[
            pltpu.SemaphoreType.DMA((1,)),
            pltpu.SemaphoreType.DMA((COLS - 1,)),
            pltpu.SemaphoreType.DMA((COLS - 1,)),
        ],
        compiler_params=pltpu.CompilerParams(collective_id=2, has_side_effects=True),
        name="xy_back",
    )(send)


def reduce_kernel(part_ref, out_ref, come, go, send_sem, recv_sem):
    base, z = z_place()
    m = z // 2
    ends = neighbours()
    half = out_ref.shape[0] // 2
    signal_all(ends)
    last = RING // 2 - 1

    def copy(way, step, chunk):
        rows = pl.ds(chunk * half, half)
        return pltpu.make_async_remote_copy(
            src_ref=go.at[way, step, rows],
            dst_ref=come.at[way, step, rows],
            send_sem=send_sem.at[way, step, chunk],
            recv_sem=recv_sem.at[way, step, chunk],
            device_id={"ep": ends[way]},
            device_id_type=MESH,
        )

    started, unread = [], {}
    for step in range(last + 1):
        for chunk in (0, 1):
            for way in (0, 1):
                if step == 0 and way != chunk:
                    continue
                ahead = RING // 2 - step
                target = (m + (ahead if way == 0 else RING - ahead)) % RING
                rows = pl.ds(chunk * half, half)
                value = part_ref[target, rows]
                earlier = unread.pop((way, step - 1, chunk), None)
                if earlier is not None:
                    earlier.wait_recv()
                    value = (
                        value.astype(jnp.float32) + come[way, step - 1, rows].astype(jnp.float32)
                    ).astype(jnp.bfloat16)
                go[way, step, rows] = value
                sent = copy(way, step, chunk)
                sent.start()
                started.append(sent)
                unread[way, step, chunk] = sent
    for chunk in (0, 1):
        rows = pl.ds(chunk * half, half)
        total = part_ref[m, rows].astype(jnp.float32)
        for way in (0, 1):
            unread.pop((way, last, chunk)).wait_recv()
            total += come[way, last, rows].astype(jnp.float32)
        out_ref[rows] = total.astype(jnp.bfloat16)
    for sent in started:
        sent.wait_send()


def z_reduce(part):
    _, rows, width = part.shape
    return pl.pallas_call(
        reduce_kernel,
        out_shape=jax.ShapeDtypeStruct((rows, width), part.dtype),
        in_specs=[pl.BlockSpec(memory_space=pltpu.VMEM)],
        out_specs=pl.BlockSpec(memory_space=pltpu.VMEM),
        scratch_shapes=[
            pltpu.VMEM((2, RING // 2, rows, width), part.dtype),
            pltpu.VMEM((2, RING // 2, rows, width), part.dtype),
            pltpu.SemaphoreType.DMA((2, RING // 2, 2)),
            pltpu.SemaphoreType.DMA((2, RING // 2, 2)),
        ],
        compiler_params=pltpu.CompilerParams(
            collective_id=3, has_side_effects=True, vmem_limit_bytes=32 << 20
        ),
        name="z_reduce",
    )(part)


def local(tokens, gates, expert_ids, slot_expert, w_in, w_out):
    rows, width = tokens.shape
    top = expert_ids.shape[1]
    meta = jnp.concatenate([expert_ids.astype(jnp.float32), gates], axis=1)
    meta = meta.reshape(rows * 2 * top // 128, 128)
    all_tokens, all_meta = z_gather(tokens, meta)
    all_meta = all_meta.reshape(RING * rows, 2 * top)
    ids, weights = all_meta[:, :top], all_meta[:, top:]
    z_block = lax.axis_index("ep") % Z // GROUP
    here = lax.dynamic_index_in_dim(
        slot_expert.reshape(COLS, Z // GROUP), z_block, 1, keepdims=False
    ).astype(jnp.float32)
    same = ids[None, :, :] == here[:, None, None]
    gate = jnp.sum(jnp.where(same, weights[None], 0.0), axis=2)
    chosen = jnp.any(same, axis=2)
    before = jnp.tril(jnp.ones((rows, rows), jnp.bfloat16), -1)
    rank = jnp.einsum(
        "cbs,ts->cbt",
        chosen.reshape(COLS, RING, rows).astype(jnp.bfloat16),
        before,
        preferred_element_type=jnp.float32,
    ).astype(jnp.int32)
    slot = rank + CAPE * jnp.arange(RING, dtype=jnp.int32)[None, :, None]
    slot = jnp.where(chosen, slot.reshape(COLS, RING * rows), -1)
    slots = RING * CAPE
    hit = jnp.arange(slots, dtype=jnp.int32)[None, :, None] == slot[:, None, :]
    pick = hit.astype(jnp.bfloat16).reshape(COLS * slots, RING * rows)
    send = jnp.dot(
        pick, all_tokens.reshape(RING * rows, width), preferred_element_type=jnp.float32
    ).astype(jnp.bfloat16)
    recv, win2, wout2 = xy_out(send.reshape(COLS, slots, width), w_in, w_out)
    recv = recv.reshape(COLS * slots, width)
    ff = win2.shape[1] * win2.shape[2]
    both = lax.dot_general(
        recv,
        win2.reshape(2 * ff, width),
        (((1,), (1,)), ((), ())),
        preferred_element_type=jnp.float32,
    )
    hidden = (jax.nn.silu(both[:, :ff]) * both[:, ff:]).astype(jnp.bfloat16)
    produced = jnp.dot(
        hidden, wout2.reshape(ff, width), preferred_element_type=jnp.float32
    ).astype(jnp.bfloat16)
    back = xy_back(produced.reshape(COLS, slots, width)).reshape(COLS * slots, width)
    high = lax.reduce_precision(gate, 8, 7)
    low = gate - high
    zero = jnp.zeros((), jnp.float32)
    part = jnp.zeros((RING * rows, width), jnp.float32)
    for piece in (high, low):
        mix = jnp.where(hit, piece[:, None, :], zero).astype(jnp.bfloat16)
        part += lax.dot_general(
            mix.reshape(COLS * slots, RING * rows),
            back,
            (((0,), (0,)), ((), ())),
            preferred_element_type=jnp.float32,
        )
    return z_reduce(part.astype(jnp.bfloat16).reshape(RING, rows, width))


def solution(mesh):
    return jax.shard_map(
        local,
        mesh=mesh,
        in_specs=(
            P(("dp", "ep"), None),
            P(("dp", "ep"), None),
            P(("dp", "ep"), None),
            P("dp"),
            P(("dp", "ep"), None, None, None),
            P(("dp", "ep"), None, None),
        ),
        out_specs=P(("dp", "ep"), None),
        check_vma=False,
    )
```

```python
import jax
import jax.numpy as jnp
from jax import lax
from jax.experimental import pallas as pl
from jax.experimental.pallas import tpu as pltpu
from jax.sharding import PartitionSpec as P

MESH = pl.DeviceIdType.MESH
GROUP = 4
CAPE = 20
Z = 16
X = 4
Y = 2
RING = Z // 2
COLS = X * Y
CHUNKS = 4


def z_place():
    me = lax.axis_index("ep")
    z = me % Z
    return me - z, z


def neighbours():
    base, z = z_place()
    return base + (z + 2) % Z, base + (z + Z - 2) % Z


def signal_all(devices):
    barrier = pltpu.get_barrier_semaphore()
    for device in devices:
        pl.semaphore_signal(barrier, inc=1, device_id={"ep": device}, device_id_type=MESH)
    pl.semaphore_wait(barrier, len(devices))


def columns():
    me = lax.axis_index("ep")
    return me // (X * Z), me // Z % X, me % Z


def column_at(y, x):
    return y % Y * X + x % X


def xy_peers():
    y, x, z = columns()
    return [
        column_at(y + ky, x + kx) * Z + z for ky in range(Y) for kx in range(X) if kx or ky
    ]


def xy_copies(send_ref, recv_ref, relay_ref, cols, send_sem, recv_sem):
    y, x, z = columns()
    mine = column_at(y, x)
    half = send_ref.shape[1] // 2

    def remote(k, src, dst, column):
        return pltpu.make_async_remote_copy(
            src_ref=src,
            dst_ref=dst,
            send_sem=send_sem.at[k],
            recv_sem=recv_sem.at[k],
            device_id={"ep": column * Z + z},
            device_id_type=MESH,
        )

    relays, forwards, direct = [], [], []
    for way, step in ((0, 1), (1, X - 1)):
        rows = pl.ds(way * half, half)
        for ky in range(Y):
            k = 2 * way + ky
            slot = relay_ref.at[way, ky, :, cols]
            relays.append(
                remote(
                    k, send_ref.at[column_at(y + ky, x + 2), rows, cols], slot, column_at(y, x + step)
                )
            )
            forwards.append(
                remote(
                    4 + k,
                    slot,
                    recv_ref.at[column_at(y, x + X - step), rows, cols],
                    column_at(y + ky, x + step),
                )
            )
    for k, (ky, kx) in enumerate(((1, 1), (1, 3), (1, 0), (0, 1), (0, 3))):
        other = column_at(y + ky, x + kx)
        direct.append(
            remote(8 + k, send_ref.at[other, :, cols], recv_ref.at[mine, :, cols], other)
        )
    return relays, forwards, direct


XY_COPIES = 13


def out_kernel(
    tok_ref, ids_ref, gates_ref, expert_ref, win_ref, wout_ref,
    recv_ref, meta_ref, win2_ref, wout2_ref,
    held, table, pick, send, relay,
    own_sem, zs_sem, zr_sem, ms_sem, mr_sem, xs_sem, xr_sem, keep_sem, ws_sem, wr_sem, wl_sem,
):
    base, z = z_place()
    m, member = z // 2, z % 2
    ends = neighbours()
    rows, width = tok_ref.shape
    slots = pick.shape[1]
    part = width // CHUNKS
    y, x, _ = columns()
    mine = column_at(y, x)
    partner = mine * Z + z + 1 - 2 * member
    ring = [base + (z + 2 * k) % Z for k in range(1, RING)]
    signal_all(ring + [partner] + xy_peers())

    own = pltpu.make_async_copy(tok_ref, held.at[pl.ds(m * rows, rows)], own_sem.at[0])
    own.start()
    last = RING // 2 - 1
    z_sent, started = {}, []

    def z_copy(way, step, chunk):
        owner = (m + (RING - step if way == 0 else step)) % RING
        count = rows // 2 if step == last else rows
        first = way * (rows // 2) if step == last else 0
        cols = pl.ds(chunk * part, part)
        there = held.at[pl.ds(owner * rows + first, count), cols]
        return pltpu.make_async_remote_copy(
            src_ref=tok_ref.at[:, cols] if step == 0 else there,
            dst_ref=there,
            send_sem=zs_sem.at[way, step, chunk],
            recv_sem=zr_sem.at[way, step, chunk],
            device_id={"ep": ends[way]},
            device_id_type=MESH,
        )

    def z_go(chunk, step):
        for way in (0, 1):
            if step:
                z_sent[way, step - 1, chunk].wait_recv()
            sent = z_copy(way, step, chunk)
            sent.start()
            z_sent[way, step, chunk] = sent
            started.append(sent)

    z_go(0, 0)

    chosen = jnp.zeros((Z // GROUP * COLS, rows), jnp.float32)
    gate = jnp.zeros((Z // GROUP * COLS, rows), jnp.float32)
    for k in range(ids_ref.shape[0]):
        same = ids_ref[pl.ds(k, 1), :] == expert_ref[...]
        chosen += jnp.where(same, 1.0, 0.0)
        gate += jnp.where(same, gates_ref[pl.ds(k, 1), :], 0.0)
    earlier = lax.broadcasted_iota(jnp.int32, (rows, rows), 0) < lax.broadcasted_iota(
        jnp.int32, (rows, rows), 1
    )
    rank = jnp.dot(
        chosen.astype(jnp.bfloat16),
        jnp.where(earlier, 1.0, 0.0).astype(jnp.bfloat16),
        preferred_element_type=jnp.float32,
    )
    slot = jnp.where(chosen > 0.5, rank + (m * CAPE).astype(jnp.float32), -1.0)
    table[:, 0] = jnp.concatenate([slot, slot], axis=1).reshape(Z // GROUP, COLS, 2 * rows)
    table[:, 1] = jnp.concatenate([gate, gate], axis=1).reshape(Z // GROUP, COLS, 2 * rows)
    metas = []
    for k in range(1, RING):
        other = (m + k) % RING
        metas.append(
            pltpu.make_async_remote_copy(
                src_ref=table.at[other // 2],
                dst_ref=meta_ref.at[m],
                send_sem=ms_sem.at[k - 1],
                recv_sem=mr_sem.at[k - 1],
                device_id={"ep": base + (z + 2 * k) % Z},
                device_id_type=MESH,
            )
        )
        metas[-1].start()
    meta_ref[m] = table[m // 2]

    pieces = [
        (win_ref.at[0, 0], win2_ref.at[0, member]),
        (win_ref.at[0, 1], win2_ref.at[1, member]),
        (wout_ref.at[0], wout2_ref.at[member]),
    ]
    weights, kept = [], []
    exchanges = []
    for chunk in range(CHUNKS):
        cols = pl.ds(chunk * part, part)
        z_go(chunk, 1)
        z_go(chunk, 2)
        if chunk + 1 < CHUNKS:
            z_go(chunk + 1, 0)
        z_go(chunk, 3)
        if chunk == 0:
            for sent in metas:
                sent.wait_recv()
            for pair in range(RING // 2):
                left = lax.broadcasted_iota(jnp.int32, (COLS, 2 * rows), 1) < rows
                both = jnp.where(left, meta_ref[2 * pair, 0], meta_ref[2 * pair + 1, 0])
                place = lax.broadcasted_iota(jnp.int32, (slots, 2 * rows), 0).astype(jnp.float32)
                for column in range(COLS):
                    hit = place == jnp.broadcast_to(both[column : column + 1], place.shape)
                    pick[column, :, pl.ds(pair * 2 * rows, 2 * rows)] = jnp.where(
                        hit, 1.0, 0.0
                    ).astype(jnp.bfloat16)
            own.wait()
        else:
            relays, forwards, _ = exchanges[chunk - 1]
            for came, sent in zip(relays, forwards):
                came.wait_recv()
                sent.start()
        for way in (0, 1):
            z_sent[way, last, chunk].wait_recv()

        @pl.loop(0, COLS)
        def _(column):
            send[column, :, cols] = jnp.dot(
                pick[column], held[:, cols], preferred_element_type=jnp.float32
            ).astype(jnp.bfloat16)

        relays, forwards, direct = xy_copies(
            send, recv_ref, relay, cols, xs_sem.at[chunk], xr_sem.at[chunk]
        )
        for sent in relays + direct:
            sent.start()
        exchanges.append((relays, forwards, direct))
        kept.append(
            pltpu.make_async_copy(
                send.at[mine, :, cols], recv_ref.at[mine, :, cols], keep_sem.at[chunk]
            )
        )
        kept[-1].start()
        if chunk:
            k = chunk - 1
            src, dst = pieces[k]
            weights.append(
                pltpu.make_async_remote_copy(
                    src_ref=src,
                    dst_ref=dst,
                    send_sem=ws_sem.at[k],
                    recv_sem=wr_sem.at[k],
                    device_id={"ep": partner},
                    device_id_type=MESH,
                )
            )
            weights[-1].start()
            kept.append(pltpu.make_async_copy(src, dst, wl_sem.at[k]))
            kept[-1].start()
    relays, forwards, _ = exchanges[-1]
    for came, sent in zip(relays, forwards):
        came.wait_recv()
        sent.start()
    for relays, forwards, direct in exchanges:
        for sent in direct + forwards:
            sent.wait_recv()
        for sent in relays + forwards + direct:
            sent.wait_send()
    for sent in started + metas:
        sent.wait_send()
    for sent in weights:
        sent.wait()
    for piece in kept:
        piece.wait()


def dispatch(tokens, ids, gates, expert, w_in, w_out):
    rows, width = tokens.shape
    _, two, ff, _ = w_in.shape
    slots = RING * CAPE
    steps = RING // 2
    dma = pltpu.SemaphoreType.DMA
    return pl.pallas_call(
        out_kernel,
        out_shape=(
            jax.ShapeDtypeStruct((COLS, slots, width), tokens.dtype),
            jax.ShapeDtypeStruct((RING, 2, COLS, 2 * rows), jnp.float32),
            jax.ShapeDtypeStruct((two, 2, ff, width), w_in.dtype),
            jax.ShapeDtypeStruct((2, ff, width), w_out.dtype),
        ),
        in_specs=[pl.BlockSpec(memory_space=pl.ANY)]
        + [pl.BlockSpec(memory_space=pltpu.VMEM)] * 3
        + [pl.BlockSpec(memory_space=pl.ANY)] * 2,
        out_specs=[
            pl.BlockSpec(memory_space=pl.ANY),
            pl.BlockSpec(memory_space=pltpu.VMEM),
            pl.BlockSpec(memory_space=pl.ANY),
            pl.BlockSpec(memory_space=pl.ANY),
        ],
        scratch_shapes=[
            pltpu.VMEM((RING * rows, width), tokens.dtype),
            pltpu.VMEM((Z // GROUP, 2, COLS, 2 * rows), jnp.float32),
            pltpu.VMEM((COLS, slots, RING * rows), jnp.bfloat16),
            pltpu.VMEM((COLS, slots, width), tokens.dtype),
            pltpu.VMEM((2, Y, slots // 2, width), tokens.dtype),
            dma((1,)),
            dma((2, steps, CHUNKS)),
            dma((2, steps, CHUNKS)),
            dma((RING - 1,)),
            dma((RING - 1,)),
            dma((CHUNKS, XY_COPIES)),
            dma((CHUNKS, XY_COPIES)),
            dma((CHUNKS,)),
            dma((3,)),
            dma((3,)),
            dma((3,)),
        ],
        compiler_params=pltpu.CompilerParams(
            collective_id=1, has_side_effects=True, vmem_limit_bytes=40 << 20
        ),
        name="dispatch",
    )(tokens, ids, gates, expert, w_in, w_out)


def back_kernel(send_ref, recv_ref, relay, local_sem, send_sem, recv_sem):
    y, x, _ = columns()
    mine = column_at(y, x)
    signal_all(xy_peers())
    own = pltpu.make_async_copy(send_ref.at[mine], recv_ref.at[mine], local_sem.at[0])
    cols = pl.ds(0, send_ref.shape[2])
    relays, forwards, direct = xy_copies(send_ref, recv_ref, relay, cols, send_sem, recv_sem)
    for sent in relays + direct:
        sent.start()
    own.start()
    for came, sent in zip(relays, forwards):
        came.wait_recv()
        sent.start()
    for sent in direct + forwards:
        sent.wait_recv()
    for sent in relays + forwards + direct:
        sent.wait_send()
    own.wait()


def xy_back(send):
    _, slots, width = send.shape
    return pl.pallas_call(
        back_kernel,
        out_shape=jax.ShapeDtypeStruct(send.shape, send.dtype),
        in_specs=[pl.BlockSpec(memory_space=pl.ANY)],
        out_specs=pl.BlockSpec(memory_space=pl.ANY),
        scratch_shapes=[
            pltpu.VMEM((2, Y, slots // 2, width), send.dtype),
            pltpu.SemaphoreType.DMA((1,)),
            pltpu.SemaphoreType.DMA((XY_COPIES,)),
            pltpu.SemaphoreType.DMA((XY_COPIES,)),
        ],
        compiler_params=pltpu.CompilerParams(collective_id=2, has_side_effects=True),
        name="xy_back",
    )(send)


def reduce_kernel(part_ref, out_ref, come, go, send_sem, recv_sem):
    base, z = z_place()
    m = z // 2
    ends = neighbours()
    half = out_ref.shape[0] // 2
    signal_all(ends)
    last = RING // 2 - 1

    def copy(way, step, chunk):
        rows = pl.ds(chunk * half, half)
        return pltpu.make_async_remote_copy(
            src_ref=go.at[way, step, rows],
            dst_ref=come.at[way, step, rows],
            send_sem=send_sem.at[way, step, chunk],
            recv_sem=recv_sem.at[way, step, chunk],
            device_id={"ep": ends[way]},
            device_id_type=MESH,
        )

    started, unread = [], {}
    for step in range(last + 1):
        for chunk in (0, 1):
            for way in (0, 1):
                if step == 0 and way != chunk:
                    continue
                ahead = RING // 2 - step
                target = (m + (ahead if way == 0 else RING - ahead)) % RING
                rows = pl.ds(chunk * half, half)
                value = part_ref[target, rows]
                earlier = unread.pop((way, step - 1, chunk), None)
                if earlier is not None:
                    earlier.wait_recv()
                    value = (
                        value.astype(jnp.float32) + come[way, step - 1, rows].astype(jnp.float32)
                    ).astype(jnp.bfloat16)
                go[way, step, rows] = value
                sent = copy(way, step, chunk)
                sent.start()
                started.append(sent)
                unread[way, step, chunk] = sent
    for chunk in (0, 1):
        rows = pl.ds(chunk * half, half)
        total = part_ref[m, rows].astype(jnp.float32)
        for way in (0, 1):
            unread.pop((way, last, chunk)).wait_recv()
            total += come[way, last, rows].astype(jnp.float32)
        out_ref[rows] = total.astype(jnp.bfloat16)
    for sent in started:
        sent.wait_send()


def z_reduce(part):
    _, rows, width = part.shape
    return pl.pallas_call(
        reduce_kernel,
        out_shape=jax.ShapeDtypeStruct((rows, width), part.dtype),
        in_specs=[pl.BlockSpec(memory_space=pltpu.VMEM)],
        out_specs=pl.BlockSpec(memory_space=pltpu.VMEM),
        scratch_shapes=[
            pltpu.VMEM((2, RING // 2, rows, width), part.dtype),
            pltpu.VMEM((2, RING // 2, rows, width), part.dtype),
            pltpu.SemaphoreType.DMA((2, RING // 2, 2)),
            pltpu.SemaphoreType.DMA((2, RING // 2, 2)),
        ],
        compiler_params=pltpu.CompilerParams(
            collective_id=3, has_side_effects=True, vmem_limit_bytes=32 << 20
        ),
        name="z_reduce",
    )(part)


def local(tokens, gates, expert_ids, slot_expert, w_in, w_out):
    rows, width = tokens.shape
    expert = slot_expert.reshape(COLS, Z // GROUP).T.reshape(-1, 1)
    recv, meta, win2, wout2 = dispatch(tokens, expert_ids.T, gates.T, expert, w_in, w_out)
    slots = RING * CAPE
    recv = recv.reshape(COLS * slots, width)
    ff = win2.shape[1] * win2.shape[2]
    both = lax.dot_general(
        recv,
        win2.reshape(2 * ff, width),
        (((1,), (1,)), ((), ())),
        preferred_element_type=jnp.float32,
    )
    hidden = (jax.nn.silu(both[:, :ff]) * both[:, ff:]).astype(jnp.bfloat16)
    produced = jnp.dot(
        hidden, wout2.reshape(ff, width), preferred_element_type=jnp.float32
    ).astype(jnp.bfloat16)
    back = xy_back(produced.reshape(COLS, slots, width)).reshape(COLS * slots, width)
    meta = meta[..., :rows].transpose(1, 2, 0, 3).reshape(2, COLS, RING * rows)
    slot, gate = meta[0].astype(jnp.int32), meta[1]
    hit = jnp.arange(slots, dtype=jnp.int32)[None, :, None] == slot[:, None, :]
    high = lax.reduce_precision(gate, 8, 7)
    low = gate - high
    zero = jnp.zeros((), jnp.float32)
    part = jnp.zeros((RING * rows, width), jnp.float32)
    for piece in (high, low):
        mix = jnp.where(hit, piece[:, None, :], zero).astype(jnp.bfloat16)
        part += lax.dot_general(
            mix.reshape(COLS * slots, RING * rows),
            back,
            (((0,), (0,)), ((), ())),
            preferred_element_type=jnp.float32,
        )
    return z_reduce(part.astype(jnp.bfloat16).reshape(RING, rows, width))


def solution(mesh):
    return jax.shard_map(
        local,
        mesh=mesh,
        in_specs=(
            P(("dp", "ep"), None),
            P(("dp", "ep"), None),
            P(("dp", "ep"), None),
            P("dp"),
            P(("dp", "ep"), None, None, None),
            P(("dp", "ep"), None, None),
        ),
        out_specs=P(("dp", "ep"), None),
        check_vma=False,
    )
```

```python
import jax
import jax.numpy as jnp
from jax import lax
from jax.experimental import pallas as pl
from jax.experimental.pallas import tpu as pltpu
from jax.sharding import PartitionSpec as P

MESH = pl.DeviceIdType.MESH
GROUP = 4
CAPE = 20
Z = 16
X = 4
Y = 2
RING = Z // 2
COLS = X * Y
CHUNKS = 4


def z_place():
    me = lax.axis_index("ep")
    z = me % Z
    return me - z, z


def neighbours():
    base, z = z_place()
    return base + (z + 2) % Z, base + (z + Z - 2) % Z


def signal_all(devices):
    barrier = pltpu.get_barrier_semaphore()
    for device in devices:
        pl.semaphore_signal(barrier, inc=1, device_id={"ep": device}, device_id_type=MESH)
    pl.semaphore_wait(barrier, len(devices))


def columns():
    me = lax.axis_index("ep")
    return me // (X * Z), me // Z % X, me % Z


def column_at(y, x):
    return y % Y * X + x % X


def xy_peers():
    y, x, z = columns()
    return [
        column_at(y + ky, x + kx) * Z + z for ky in range(Y) for kx in range(X) if kx or ky
    ]


def xy_copies(send_ref, recv_ref, relay_ref, cols, send_sem, recv_sem):
    y, x, z = columns()
    mine = column_at(y, x)
    half = send_ref.shape[1] // 2

    def remote(k, src, dst, column):
        return pltpu.make_async_remote_copy(
            src_ref=src,
            dst_ref=dst,
            send_sem=send_sem.at[k],
            recv_sem=recv_sem.at[k],
            device_id={"ep": column * Z + z},
            device_id_type=MESH,
        )

    relays, forwards, direct = [], [], []
    for way, step in ((0, 1), (1, X - 1)):
        rows = pl.ds(way * half, half)
        for ky in range(Y):
            k = 2 * way + ky
            slot = relay_ref.at[way, ky, :, cols]
            relays.append(
                remote(
                    k, send_ref.at[column_at(y + ky, x + 2), rows, cols], slot, column_at(y, x + step)
                )
            )
            forwards.append(
                remote(
                    4 + k,
                    slot,
                    recv_ref.at[column_at(y, x + X - step), rows, cols],
                    column_at(y + ky, x + step),
                )
            )
    for k, (ky, kx) in enumerate(((1, 1), (1, 3), (1, 0), (0, 1), (0, 3))):
        other = column_at(y + ky, x + kx)
        direct.append(
            remote(8 + k, send_ref.at[other, :, cols], recv_ref.at[mine, :, cols], other)
        )
    return relays, forwards, direct


XY_COPIES = 13


def out_kernel(
    tok_ref, ids_ref, gates_ref, expert_ref, win_ref, wout_ref,
    recv_ref, meta_ref, win2_ref, wout2_ref,
    held, table, pick, send, relay,
    own_sem, zs_sem, zr_sem, ms_sem, mr_sem, xs_sem, xr_sem, keep_sem, ws_sem, wr_sem, wl_sem,
):
    base, z = z_place()
    m, member = z // 2, z % 2
    ends = neighbours()
    rows, width = tok_ref.shape
    slots = pick.shape[1]
    part = width // CHUNKS
    y, x, _ = columns()
    mine = column_at(y, x)
    partner = mine * Z + z + 1 - 2 * member
    ring = [base + (z + 2 * k) % Z for k in range(1, RING)]
    signal_all(ring + [partner] + xy_peers())

    own = pltpu.make_async_copy(tok_ref, held.at[pl.ds(m * rows, rows)], own_sem.at[0])
    own.start()
    last = RING // 2 - 1
    z_sent, started = {}, []

    def z_copy(way, step, chunk):
        owner = (m + (RING - step if way == 0 else step)) % RING
        count = rows // 2 if step == last else rows
        first = way * (rows // 2) if step == last else 0
        cols = pl.ds(chunk * part, part)
        there = held.at[pl.ds(owner * rows + first, count), cols]
        return pltpu.make_async_remote_copy(
            src_ref=tok_ref.at[:, cols] if step == 0 else there,
            dst_ref=there,
            send_sem=zs_sem.at[way, step, chunk],
            recv_sem=zr_sem.at[way, step, chunk],
            device_id={"ep": ends[way]},
            device_id_type=MESH,
        )

    def z_go(chunk, step):
        for way in (0, 1):
            if step:
                z_sent[way, step - 1, chunk].wait_recv()
            sent = z_copy(way, step, chunk)
            sent.start()
            z_sent[way, step, chunk] = sent
            started.append(sent)

    z_go(0, 0)

    chosen = jnp.zeros((Z // GROUP * COLS, rows), jnp.float32)
    gate = jnp.zeros((Z // GROUP * COLS, rows), jnp.float32)
    for k in range(ids_ref.shape[0]):
        same = ids_ref[pl.ds(k, 1), :] == expert_ref[...]
        chosen += jnp.where(same, 1.0, 0.0)
        gate += jnp.where(same, gates_ref[pl.ds(k, 1), :], 0.0)
    earlier = lax.broadcasted_iota(jnp.int32, (rows, rows), 0) < lax.broadcasted_iota(
        jnp.int32, (rows, rows), 1
    )
    rank = jnp.dot(
        chosen.astype(jnp.bfloat16),
        jnp.where(earlier, 1.0, 0.0).astype(jnp.bfloat16),
        preferred_element_type=jnp.float32,
    )
    slot = jnp.where(chosen > 0.5, rank + (m * CAPE).astype(jnp.float32), -1.0)
    table[:, 0] = jnp.concatenate([slot, slot], axis=1).reshape(Z // GROUP, COLS, 2 * rows)
    table[:, 1] = jnp.concatenate([gate, gate], axis=1).reshape(Z // GROUP, COLS, 2 * rows)
    metas = []
    for k in range(1, RING):
        other = (m + k) % RING
        metas.append(
            pltpu.make_async_remote_copy(
                src_ref=table.at[other // 2],
                dst_ref=meta_ref.at[m],
                send_sem=ms_sem.at[k - 1],
                recv_sem=mr_sem.at[k - 1],
                device_id={"ep": base + (z + 2 * k) % Z},
                device_id_type=MESH,
            )
        )
        metas[-1].start()
    meta_ref[m] = table[m // 2]

    pieces = [
        (win_ref.at[0, 0], win2_ref.at[0, member]),
        (win_ref.at[0, 1], win2_ref.at[1, member]),
        (wout_ref.at[0], wout2_ref.at[member]),
    ]
    weights, kept = [], []
    exchanges = []
    for chunk in range(CHUNKS):
        cols = pl.ds(chunk * part, part)
        z_go(chunk, 1)
        z_go(chunk, 2)
        if chunk + 1 < CHUNKS:
            z_go(chunk + 1, 0)
        z_go(chunk, 3)
        if chunk == 0:
            for sent in metas:
                sent.wait_recv()
            for pair in range(RING // 2):
                left = lax.broadcasted_iota(jnp.int32, (COLS, 2 * rows), 1) < rows
                both = jnp.where(left, meta_ref[2 * pair, 0], meta_ref[2 * pair + 1, 0])
                place = lax.broadcasted_iota(jnp.int32, (slots, 2 * rows), 0).astype(jnp.float32)
                for column in range(COLS):
                    hit = place == jnp.broadcast_to(both[column : column + 1], place.shape)
                    pick[column, :, pl.ds(pair * 2 * rows, 2 * rows)] = jnp.where(
                        hit, 1.0, 0.0
                    ).astype(jnp.bfloat16)
            own.wait()
        else:
            relays, forwards, _ = exchanges[chunk - 1]
            for came, sent in zip(relays, forwards):
                came.wait_recv()
                sent.start()
        for way in (0, 1):
            z_sent[way, last, chunk].wait_recv()

        @pl.loop(0, COLS)
        def _(column):
            send[column, :, cols] = jnp.dot(
                pick[column], held[:, cols], preferred_element_type=jnp.float32
            ).astype(jnp.bfloat16)

        relays, forwards, direct = xy_copies(
            send, recv_ref, relay, cols, xs_sem.at[chunk], xr_sem.at[chunk]
        )
        for sent in relays + direct:
            sent.start()
        exchanges.append((relays, forwards, direct))
        kept.append(
            pltpu.make_async_copy(
                send.at[mine, :, cols], recv_ref.at[mine, :, cols], keep_sem.at[chunk]
            )
        )
        kept[-1].start()
        if chunk:
            k = chunk - 1
            src, dst = pieces[k]
            weights.append(
                pltpu.make_async_remote_copy(
                    src_ref=src,
                    dst_ref=dst,
                    send_sem=ws_sem.at[k],
                    recv_sem=wr_sem.at[k],
                    device_id={"ep": partner},
                    device_id_type=MESH,
                )
            )
            weights[-1].start()
            kept.append(pltpu.make_async_copy(src, dst, wl_sem.at[k]))
            kept[-1].start()
    relays, forwards, _ = exchanges[-1]
    for came, sent in zip(relays, forwards):
        came.wait_recv()
        sent.start()
    for relays, forwards, direct in exchanges:
        for sent in direct + forwards:
            sent.wait_recv()
        for sent in relays + forwards + direct:
            sent.wait_send()
    for sent in started + metas:
        sent.wait_send()
    for sent in weights:
        sent.wait()
    for piece in kept:
        piece.wait()


def dispatch(tokens, ids, gates, expert, w_in, w_out):
    rows, width = tokens.shape
    _, two, ff, _ = w_in.shape
    slots = RING * CAPE
    steps = RING // 2
    dma = pltpu.SemaphoreType.DMA
    return pl.pallas_call(
        out_kernel,
        out_shape=(
            jax.ShapeDtypeStruct((COLS, slots, width), tokens.dtype),
            jax.ShapeDtypeStruct((RING, 2, COLS, 2 * rows), jnp.float32),
            jax.ShapeDtypeStruct((two, 2, ff, width), w_in.dtype),
            jax.ShapeDtypeStruct((2, ff, width), w_out.dtype),
        ),
        in_specs=[pl.BlockSpec(memory_space=pl.ANY)]
        + [pl.BlockSpec(memory_space=pltpu.VMEM)] * 3
        + [pl.BlockSpec(memory_space=pl.ANY)] * 2,
        out_specs=[
            pl.BlockSpec(memory_space=pl.ANY),
            pl.BlockSpec(memory_space=pltpu.VMEM),
            pl.BlockSpec(memory_space=pl.ANY),
            pl.BlockSpec(memory_space=pl.ANY),
        ],
        scratch_shapes=[
            pltpu.VMEM((RING * rows, width), tokens.dtype),
            pltpu.VMEM((Z // GROUP, 2, COLS, 2 * rows), jnp.float32),
            pltpu.VMEM((COLS, slots, RING * rows), jnp.bfloat16),
            pltpu.VMEM((COLS, slots, width), tokens.dtype),
            pltpu.VMEM((2, Y, slots // 2, width), tokens.dtype),
            dma((1,)),
            dma((2, steps, CHUNKS)),
            dma((2, steps, CHUNKS)),
            dma((RING - 1,)),
            dma((RING - 1,)),
            dma((CHUNKS, XY_COPIES)),
            dma((CHUNKS, XY_COPIES)),
            dma((CHUNKS,)),
            dma((3,)),
            dma((3,)),
            dma((3,)),
        ],
        compiler_params=pltpu.CompilerParams(
            collective_id=1, has_side_effects=True, vmem_limit_bytes=40 << 20
        ),
        name="dispatch",
    )(tokens, ids, gates, expert, w_in, w_out)


def back_kernel(
    hidden_ref, wout_ref, meta_ref, out_ref,
    send, back, relay, mix, part, come, go, zs_sem, zr_sem, xs_sem, xr_sem,
):
    base, z = z_place()
    m = z // 2
    ends = neighbours()
    rows, width = out_ref.shape
    slots = send.shape[1]
    size = width // CHUNKS
    half = rows // 2
    last = RING // 2 - 1
    y, x, _ = columns()
    mine = column_at(y, x)
    signal_all(list(ends) + xy_peers())
    exchanges, started, z_sent = [], [], {}

    def span(chunk):
        return pl.ds(chunk * size, size)

    def produce(chunk):
        cols = span(chunk)

        @pl.loop(0, COLS)
        def _(column):
            send[column, :, cols] = jnp.dot(
                hidden_ref[column], wout_ref[:, cols], preferred_element_type=jnp.float32
            ).astype(jnp.bfloat16)

        copies = xy_copies(send, back, relay, cols, xs_sem.at[chunk], xr_sem.at[chunk])
        for sent in copies[0] + copies[2]:
            sent.start()
        exchanges.append(copies)
        back[mine, :, cols] = send[mine, :, cols]

    def forward(chunk):
        relays, forwards, _ = exchanges[chunk]
        for came, sent in zip(relays, forwards):
            came.wait_recv()
            sent.start()

    def build_mix():
        for pair in range(RING // 2):
            left = lax.broadcasted_iota(jnp.int32, (COLS, 2 * rows), 1) < rows
            slot = jnp.where(left, meta_ref[2 * pair, 0], meta_ref[2 * pair + 1, 0])
            gate = jnp.where(left, meta_ref[2 * pair, 1], meta_ref[2 * pair + 1, 1])
            first = lax.broadcasted_iota(jnp.int32, slot.shape, 0) * slots
            slot = jnp.where(slot < 0.0, -1.0, slot + first.astype(jnp.float32)).T
            gate = gate.T
            high = gate.astype(jnp.bfloat16).astype(jnp.float32)
            low = gate - high
            for lane in range(0, COLS * slots, 128):
                place = lax.broadcasted_iota(jnp.int32, (2 * rows, 128), 1) + lane
                place = place.astype(jnp.float32)
                tops = jnp.zeros(place.shape, jnp.float32)
                rest = jnp.zeros(place.shape, jnp.float32)
                for column in range(lane // slots, (lane + 127) // slots + 1):
                    hit = place == slot[:, column : column + 1]
                    tops += jnp.where(hit, high[:, column : column + 1], 0.0)
                    rest += jnp.where(hit, low[:, column : column + 1], 0.0)
                here = pl.ds(pair * 2 * rows, 2 * rows), pl.ds(lane, 128)
                mix[0, here[0], here[1]] = tops.astype(jnp.bfloat16)
                mix[1, here[0], here[1]] = rest.astype(jnp.bfloat16)

    def merge(chunk):
        cols = span(chunk)
        _, forwards, direct = exchanges[chunk]
        for sent in direct + forwards:
            sent.wait_recv()
        tile = 256

        @pl.loop(0, RING * rows // tile)
        def _(step):
            here = pl.ds(pl.multiple_of(step * tile, tile), tile)
            values = back[:, :, cols].reshape(COLS * slots, size)
            part[here, cols] = jnp.dot(
                mix[0, here], values, preferred_element_type=jnp.float32
            ) + jnp.dot(mix[1, here], values, preferred_element_type=jnp.float32)

    def reduce_step(chunk, step):
        cols = span(chunk)
        for way in (0, 1):
            ahead = RING // 2 - step
            target = (m + (ahead if way == 0 else RING - ahead)) % RING
            count = half if step == 0 else rows
            first = way * half if step == 0 else 0
            value = part[pl.ds(target * rows + first, count), cols]
            local = pl.ds(first, count)
            if step == 0:
                go[way, step, local, cols] = value.astype(jnp.bfloat16)
            else:
                z_sent[way, step - 1, chunk].wait_recv()
                if step == 1:
                    touched = pl.ds(way * half, half)
                    other = (1 - way) * half
                    arrived = come[way, 0, touched, cols].astype(jnp.float32)
                    go[way, 1, touched, cols] = (
                        value[way * half : way * half + half] + arrived
                    ).astype(jnp.bfloat16)
                    go[way, 1, pl.ds(other, half), cols] = value[other : other + half].astype(
                        jnp.bfloat16
                    )
                else:
                    arrived = come[way, step - 1, :, cols].astype(jnp.float32)
                    go[way, step, :, cols] = (value + arrived).astype(jnp.bfloat16)
            sent = pltpu.make_async_remote_copy(
                src_ref=go.at[way, step, local, cols],
                dst_ref=come.at[way, step, local, cols],
                send_sem=zs_sem.at[way, step, chunk],
                recv_sem=zr_sem.at[way, step, chunk],
                device_id={"ep": ends[way]},
                device_id_type=MESH,
            )
            sent.start()
            started.append(sent)
            z_sent[way, step, chunk] = sent

    def finish(chunk):
        cols = span(chunk)
        total = part[pl.ds(m * rows, rows), cols]
        for way in (0, 1):
            z_sent[way, last, chunk].wait_recv()
            total += come[way, last, :, cols].astype(jnp.float32)
        out_ref[:, cols] = total.astype(jnp.bfloat16)

    produce(0)
    build_mix()
    forward(0)
    produce(1)
    for chunk in range(CHUNKS):
        merge(chunk)
        reduce_step(chunk, 0)
        if chunk:
            finish(chunk - 1)
        reduce_step(chunk, 1)
        if chunk + 1 < CHUNKS:
            forward(chunk + 1)
        if chunk + 2 < CHUNKS:
            produce(chunk + 2)
        reduce_step(chunk, 2)
        reduce_step(chunk, 3)
    finish(CHUNKS - 1)
    for relays, forwards, direct in exchanges:
        for sent in relays + forwards + direct:
            sent.wait_send()
    for sent in started:
        sent.wait_send()


def combine(hidden, w_out, meta):
    _, slots, ff = hidden.shape
    width = w_out.shape[1]
    rows = meta.shape[3] // 2
    dma = pltpu.SemaphoreType.DMA
    return pl.pallas_call(
        back_kernel,
        out_shape=jax.ShapeDtypeStruct((rows, width), w_out.dtype),
        in_specs=[pl.BlockSpec(memory_space=pltpu.VMEM)] * 3,
        out_specs=pl.BlockSpec(memory_space=pltpu.VMEM),
        scratch_shapes=[
            pltpu.VMEM((COLS, slots, width), w_out.dtype),
            pltpu.VMEM((COLS, slots, width), w_out.dtype),
            pltpu.VMEM((2, Y, slots // 2, width), w_out.dtype),
            pltpu.VMEM((2, RING * rows, COLS * slots), w_out.dtype),
            pltpu.VMEM((RING * rows, width), jnp.float32),
            pltpu.VMEM((2, RING // 2, rows, width), w_out.dtype),
            pltpu.VMEM((2, RING // 2, rows, width), w_out.dtype),
            dma((2, RING // 2, CHUNKS)),
            dma((2, RING // 2, CHUNKS)),
            dma((CHUNKS, XY_COPIES)),
            dma((CHUNKS, XY_COPIES)),
        ],
        compiler_params=pltpu.CompilerParams(
            collective_id=2, has_side_effects=True, vmem_limit_bytes=48 << 20
        ),
        name="combine",
    )(hidden, w_out, meta)


def local(tokens, gates, expert_ids, slot_expert, w_in, w_out):
    expert = slot_expert.reshape(COLS, Z // GROUP).T.reshape(-1, 1)
    recv, meta, win2, wout2 = dispatch(tokens, expert_ids.T, gates.T, expert, w_in, w_out)
    _, slots, width = recv.shape
    ff = win2.shape[1] * win2.shape[2]
    both = lax.dot_general(
        recv.reshape(COLS * slots, width),
        win2.reshape(2 * ff, width),
        (((1,), (1,)), ((), ())),
        preferred_element_type=jnp.float32,
    )
    hidden = (jax.nn.silu(both[:, :ff]) * both[:, ff:]).astype(jnp.bfloat16)
    return combine(hidden.reshape(COLS, slots, ff), wout2.reshape(ff, width), meta)


def solution(mesh):
    return jax.shard_map(
        local,
        mesh=mesh,
        in_specs=(
            P(("dp", "ep"), None),
            P(("dp", "ep"), None),
            P(("dp", "ep"), None),
            P("dp"),
            P(("dp", "ep"), None, None, None),
            P(("dp", "ep"), None, None),
        ),
        out_specs=P(("dp", "ep"), None),
        check_vma=False,
    )
```

```python
import jax
import jax.numpy as jnp
from jax import lax
from jax.experimental import pallas as pl
from jax.experimental.pallas import tpu as pltpu
from jax.sharding import PartitionSpec as P

MESH = pl.DeviceIdType.MESH
GROUP = 4
CAPE = 20
Z = 16
X = 4
Y = 2
RING = Z // 2
COLS = X * Y
CHUNKS = 4
PIECES = 4
EARLY = (0, 1, 1, 1)


def z_place():
    me = lax.axis_index("ep")
    z = me % Z
    return me - z, z


def neighbours():
    base, z = z_place()
    return base + (z + 2) % Z, base + (z + Z - 2) % Z


def signal_all(devices):
    barrier = pltpu.get_barrier_semaphore()
    for device in devices:
        pl.semaphore_signal(barrier, inc=1, device_id={"ep": device}, device_id_type=MESH)
    pl.semaphore_wait(barrier, len(devices))


def columns():
    me = lax.axis_index("ep")
    return me // (X * Z), me // Z % X, me % Z


def column_at(y, x):
    return y % Y * X + x % X


def xy_peers():
    y, x, z = columns()
    return [
        column_at(y + ky, x + kx) * Z + z for ky in range(Y) for kx in range(X) if kx or ky
    ]


def xy_copies(send_ref, recv_ref, relay_ref, send_sem, recv_sem):
    y, x, z = columns()
    mine = column_at(y, x)
    half = send_ref.shape[1] // 2

    def remote(k, src, dst, column):
        return pltpu.make_async_remote_copy(
            src_ref=src,
            dst_ref=dst,
            send_sem=send_sem.at[k],
            recv_sem=recv_sem.at[k],
            device_id={"ep": column * Z + z},
            device_id_type=MESH,
        )

    relays, forwards, direct = [], [], []
    for way, step in ((0, 1), (1, X - 1)):
        rows = pl.ds(way * half, half)
        for ky in range(Y):
            k = 2 * way + ky
            slot = relay_ref.at[k]
            relays.append(
                remote(k, send_ref.at[column_at(y + ky, x + 2), rows], slot, column_at(y, x + step))
            )
            forwards.append(
                remote(
                    4 + k,
                    slot,
                    recv_ref.at[column_at(y, x + X - step), rows],
                    column_at(y + ky, x + step),
                )
            )
    for k, (ky, kx) in enumerate(((1, 1), (1, 3), (1, 0), (0, 1), (0, 3))):
        other = column_at(y + ky, x + kx)
        direct.append(remote(8 + k, send_ref.at[other], recv_ref.at[mine], other))
    return relays, forwards, direct


XY_COPIES = 13


def layer_kernel(
    tok_ref, ids_ref, gates_ref, expert_ref, win_ref, wout_ref, out_ref,
    held, table, meta, pick, send, recv, relay, win2, wout2, act, hidden,
    back, relay2, mix, part, come, go,
    own_sem, zs_sem, zr_sem, ms_sem, mr_sem, xs_sem, xr_sem, ws_sem, wr_sem, wl_sem,
    rs_sem, rr_sem, bs_sem, br_sem,
):
    base, z = z_place()
    m, member = z // 2, z % 2
    ends = neighbours()
    rows, width = tok_ref.shape
    slots = pick.shape[1]
    size = width // CHUNKS
    half = rows // 2
    last = RING // 2 - 1
    y, x, _ = columns()
    mine = column_at(y, x)
    partner = mine * Z + z + 1 - 2 * member

    def span(chunk):
        return pl.ds(chunk * size, size)

    own = []
    for chunk in range(CHUNKS):
        own.append(
            pltpu.make_async_copy(
                tok_ref.at[:, span(chunk)], held.at[chunk, pl.ds(m * rows, rows)], own_sem.at[chunk]
            )
        )
        own[-1].start()
    ring = [base + (z + 2 * k) % Z for k in range(1, RING)]
    signal_all(ring + [partner] + xy_peers())

    z_sent, started = {}, []

    def z_go(chunk, step):
        if step == 0:
            own[chunk].wait()
        for way in (0, 1):
            if step:
                z_sent[way, step - 1, chunk].wait_recv()
            owner = (m + (RING - step if way == 0 else step)) % RING
            count = half if step == last else rows
            first = way * half if step == last else 0
            there = held.at[chunk, pl.ds(owner * rows + first, count)]
            sent = pltpu.make_async_remote_copy(
                src_ref=there,
                dst_ref=there,
                send_sem=zs_sem.at[way, step, chunk],
                recv_sem=zr_sem.at[way, step, chunk],
                device_id={"ep": ends[way]},
                device_id_type=MESH,
            )
            sent.start()
            z_sent[way, step, chunk] = sent
            started.append(sent)

    queue = sorted(
        ((chunk, step) for chunk in range(CHUNKS) for step in range(last + 1)),
        key=lambda place: (2 * place[0] + place[1], place[0]),
    )
    z_go(*queue.pop(0))

    chosen = jnp.zeros((Z // GROUP * COLS, rows), jnp.float32)
    gate = jnp.zeros((Z // GROUP * COLS, rows), jnp.float32)
    for k in range(ids_ref.shape[0]):
        same = ids_ref[pl.ds(k, 1), :] == expert_ref[...]
        chosen += jnp.where(same, 1.0, 0.0)
        gate += jnp.where(same, gates_ref[pl.ds(k, 1), :], 0.0)
    earlier = lax.broadcasted_iota(jnp.int32, (rows, rows), 0) < lax.broadcasted_iota(
        jnp.int32, (rows, rows), 1
    )
    rank = jnp.dot(
        chosen.astype(jnp.bfloat16),
        jnp.where(earlier, 1.0, 0.0).astype(jnp.bfloat16),
        preferred_element_type=jnp.float32,
    )
    slot = jnp.where(chosen > 0.5, rank + (m * CAPE).astype(jnp.float32), -1.0)
    table[:, 0] = jnp.concatenate([slot, slot], axis=1).reshape(Z // GROUP, COLS, 2 * rows)
    table[:, 1] = jnp.concatenate([gate, gate], axis=1).reshape(Z // GROUP, COLS, 2 * rows)
    metas = []
    for k in range(1, RING):
        other = (m + k) % RING
        metas.append(
            pltpu.make_async_remote_copy(
                src_ref=table.at[other // 2],
                dst_ref=meta.at[m],
                send_sem=ms_sem.at[k - 1],
                recv_sem=mr_sem.at[k - 1],
                device_id={"ep": base + (z + 2 * k) % Z},
                device_id_type=MESH,
            )
        )
        metas[-1].start()
    meta[m] = table[m // 2]

    def paired(pair, kind):
        left = lax.broadcasted_iota(jnp.int32, (COLS, 2 * rows), 1) < rows
        return jnp.where(left, meta[2 * pair, kind], meta[2 * pair + 1, kind])

    def build_pick():
        for pair in range(RING // 2):
            both = paired(pair, 0)
            place = lax.broadcasted_iota(jnp.int32, (slots, 2 * rows), 0).astype(jnp.float32)
            for column in range(COLS):
                hit = place == jnp.broadcast_to(both[column : column + 1], place.shape)
                pick[column, :, pl.ds(pair * 2 * rows, 2 * rows)] = jnp.where(
                    hit, 1.0, 0.0
                ).astype(jnp.bfloat16)

    def build_mix():
        for pair in range(RING // 2):
            slot, gate = paired(pair, 0), paired(pair, 1)
            first = lax.broadcasted_iota(jnp.int32, slot.shape, 0) * slots
            slot = jnp.where(slot < 0.0, -1.0, slot + first.astype(jnp.float32)).T
            gate = gate.T
            high = gate.astype(jnp.bfloat16).astype(jnp.float32)
            low = gate - high
            for lane in range(0, COLS * slots, 128):
                place = lax.broadcasted_iota(jnp.int32, (2 * rows, 128), 1) + lane
                place = place.astype(jnp.float32)
                tops = jnp.zeros(place.shape, jnp.float32)
                rest = jnp.zeros(place.shape, jnp.float32)
                for column in range(lane // slots, (lane + 127) // slots + 1):
                    hit = place == slot[:, column : column + 1]
                    tops += jnp.where(hit, high[:, column : column + 1], 0.0)
                    rest += jnp.where(hit, low[:, column : column + 1], 0.0)
                here = pl.ds(pair * 2 * rows, 2 * rows), pl.ds(lane, 128)
                mix[0, here[0], here[1]] = tops.astype(jnp.bfloat16)
                mix[1, here[0], here[1]] = rest.astype(jnp.bfloat16)

    ff = win_ref.shape[2]
    count = ff // PIECES
    pieces = []
    for piece in range(PIECES):
        here = pl.ds(piece * count, count)
        for side in (0, 1):
            there = pl.ds((2 * side + member) * ff + piece * count, count)
            pieces.append((win_ref.at[0, side, here], win2.at[there]))
    for piece in range(PIECES):
        here = pl.ds(piece * count, count)
        there = pl.ds(member * ff + piece * count, count)
        pieces.append((wout_ref.at[0, here], wout2.at[there]))
    weights, kept = [], []

    def weight_go(src, dst):
        k = len(weights)
        weights.append(
            pltpu.make_async_remote_copy(
                src_ref=src,
                dst_ref=dst,
                send_sem=ws_sem.at[k],
                recv_sem=wr_sem.at[k],
                device_id={"ep": partner},
                device_id_type=MESH,
            )
        )
        weights[-1].start()
        kept.append(pltpu.make_async_copy(src, dst, wl_sem.at[k]))
        kept[-1].start()

    def forward(copies):
        relays, forwards, _ = copies
        for came, sent in zip(relays, forwards):
            came.wait_recv()
            sent.start()

    exchanges = []
    for chunk in range(CHUNKS):
        while queue and 2 * queue[0][0] + queue[0][1] <= 2 * chunk + last:
            z_go(*queue.pop(0))
        for _ in range(EARLY[chunk] if queue else len(pieces)):
            weight_go(*pieces.pop(0))
        if chunk == 0:
            for sent in metas:
                sent.wait_recv()
            build_pick()
        else:
            forward(exchanges[-1])
        for way in (0, 1):
            z_sent[way, last, chunk].wait_recv()

        @pl.loop(0, COLS)
        def _(column):
            send[chunk, column] = jnp.dot(
                pick[column], held[chunk], preferred_element_type=jnp.float32
            ).astype(jnp.bfloat16)

        copies = xy_copies(
            send.at[chunk], recv.at[chunk], relay.at[chunk], xs_sem.at[chunk], xr_sem.at[chunk]
        )
        for sent in copies[0] + copies[2]:
            sent.start()
        exchanges.append(copies)
        recv[chunk, mine] = send[chunk, mine]
    build_mix()
    forward(exchanges[-1])

    tile = COLS * slots // 4
    group = COLS // 4
    for k in range(2 * PIECES):
        weights[k].wait_recv()
        kept[k].wait()
    for chunk in range(CHUNKS):
        _, forwards, direct = exchanges[chunk]
        for sent in direct + forwards:
            sent.wait_recv()

        @pl.loop(0, 4)
        def _(step):
            here = pl.ds(pl.multiple_of(step * tile, tile), tile)
            term = lax.dot_general(
                recv[chunk, pl.ds(step * group, group)].reshape(tile, size),
                win2[:, span(chunk)],
                (((1,), (1,)), ((), ())),
                preferred_element_type=jnp.float32,
            )
            if chunk:
                term += act[here]
            if chunk < CHUNKS - 1:
                act[here] = term
            else:
                side = wout2.shape[0]
                value = term[:, :side]
                value = value / (1.0 + jnp.exp(-value)) * term[:, side:]
                hidden[here] = value.astype(jnp.bfloat16)

    for relays, forwards, direct in exchanges:
        for sent in relays + forwards + direct:
            sent.wait_send()
    for k in range(2 * PIECES, 3 * PIECES):
        weights[k].wait_recv()
        kept[k].wait()

    exchanges, r_sent = [], {}

    def produce(chunk):
        @pl.loop(0, 4)
        def _(step):
            here = pl.ds(pl.multiple_of(step * tile, tile), tile)
            send[chunk, pl.ds(step * group, group)] = (
                jnp.dot(hidden[here], wout2[:, span(chunk)], preferred_element_type=jnp.float32)
                .astype(jnp.bfloat16)
                .reshape(group, slots, size)
            )

        copies = xy_copies(
            send.at[chunk], back.at[chunk], relay2.at[chunk], bs_sem.at[chunk], br_sem.at[chunk]
        )
        for sent in copies[0] + copies[2]:
            sent.start()
        exchanges.append(copies)
        back[chunk, mine] = send[chunk, mine]

    def merge(chunk):
        _, forwards, direct = exchanges[chunk]
        for sent in direct + forwards:
            sent.wait_recv()
        block = 256

        @pl.loop(0, RING * rows // block)
        def _(step):
            here = pl.ds(pl.multiple_of(step * block, block), block)
            values = back[chunk].reshape(COLS * slots, size)
            part[chunk, here] = jnp.dot(
                mix[0, here], values, preferred_element_type=jnp.float32
            ) + jnp.dot(mix[1, here], values, preferred_element_type=jnp.float32)

    def reduce_step(chunk, step):
        for way in (0, 1):
            ahead = RING // 2 - step
            target = (m + (ahead if way == 0 else RING - ahead)) % RING
            count = half if step == 0 else rows
            first = way * half if step == 0 else 0
            value = part[chunk, pl.ds(target * rows + first, count)]
            local = pl.ds(first, count)
            if step == 0:
                go[chunk, way, step, local] = value.astype(jnp.bfloat16)
            else:
                r_sent[way, step - 1, chunk].wait_recv()
                if step == 1:
                    touched = pl.ds(way * half, half)
                    other = (1 - way) * half
                    arrived = come[chunk, way, 0, touched].astype(jnp.float32)
                    go[chunk, way, 1, touched] = (
                        value[way * half : way * half + half] + arrived
                    ).astype(jnp.bfloat16)
                    go[chunk, way, 1, pl.ds(other, half)] = value[other : other + half].astype(
                        jnp.bfloat16
                    )
                else:
                    arrived = come[chunk, way, step - 1].astype(jnp.float32)
                    go[chunk, way, step] = (value + arrived).astype(jnp.bfloat16)
            sent = pltpu.make_async_remote_copy(
                src_ref=go.at[chunk, way, step, local],
                dst_ref=come.at[chunk, way, step, local],
                send_sem=rs_sem.at[way, step, chunk],
                recv_sem=rr_sem.at[way, step, chunk],
                device_id={"ep": ends[way]},
                device_id_type=MESH,
            )
            sent.start()
            started.append(sent)
            r_sent[way, step, chunk] = sent

    def finish(chunk):
        total = part[chunk, pl.ds(m * rows, rows)]
        for way in (0, 1):
            r_sent[way, last, chunk].wait_recv()
            total += come[chunk, way, last].astype(jnp.float32)
        out_ref[:, span(chunk)] = total.astype(jnp.bfloat16)

    produce(0)
    produce(1)
    forward(exchanges[0])
    for chunk in range(CHUNKS):
        merge(chunk)
        reduce_step(chunk, 0)
        if chunk + 1 < CHUNKS:
            forward(exchanges[chunk + 1])
        if chunk + 2 < CHUNKS:
            produce(chunk + 2)
        if chunk:
            reduce_step(chunk - 1, 3)
        reduce_step(chunk, 1)
        if chunk:
            finish(chunk - 1)
        reduce_step(chunk, 2)
    reduce_step(CHUNKS - 1, 3)
    finish(CHUNKS - 1)
    for relays, forwards, direct in exchanges:
        for sent in relays + forwards + direct:
            sent.wait_send()
    for sent in started + metas + weights:
        sent.wait_send()


def layer(tokens, ids, gates, expert, w_in, w_out):
    rows, width = tokens.shape
    _, two, ff, _ = w_in.shape
    slots = RING * CAPE
    steps = RING // 2
    size = width // CHUNKS
    kind = tokens.dtype
    dma = pltpu.SemaphoreType.DMA
    return pl.pallas_call(
        layer_kernel,
        out_shape=jax.ShapeDtypeStruct((rows, width), kind),
        in_specs=[pl.BlockSpec(memory_space=pl.ANY)]
        + [pl.BlockSpec(memory_space=pltpu.VMEM)] * 3
        + [pl.BlockSpec(memory_space=pl.ANY)] * 2,
        out_specs=pl.BlockSpec(memory_space=pltpu.VMEM),
        scratch_shapes=[
            pltpu.VMEM((CHUNKS, RING * rows, size), kind),
            pltpu.VMEM((Z // GROUP, 2, COLS, 2 * rows), jnp.float32),
            pltpu.VMEM((RING, 2, COLS, 2 * rows), jnp.float32),
            pltpu.VMEM((COLS, slots, RING * rows), kind),
            pltpu.VMEM((CHUNKS, COLS, slots, size), kind),
            pltpu.VMEM((CHUNKS, COLS, slots, size), kind),
            pltpu.VMEM((CHUNKS, 2 * Y, slots // 2, size), kind),
            pltpu.VMEM((two * 2 * ff, width), kind),
            pltpu.VMEM((2 * ff, width), kind),
            pltpu.VMEM((COLS * slots, two * 2 * ff), jnp.float32),
            pltpu.VMEM((COLS * slots, 2 * ff), kind),
            pltpu.VMEM((CHUNKS, COLS, slots, size), kind),
            pltpu.VMEM((CHUNKS, 2 * Y, slots // 2, size), kind),
            pltpu.VMEM((2, RING * rows, COLS * slots), kind),
            pltpu.VMEM((CHUNKS, RING * rows, size), jnp.float32),
            pltpu.VMEM((CHUNKS, 2, steps, rows, size), kind),
            pltpu.VMEM((CHUNKS, 2, steps, rows, size), kind),
            dma((CHUNKS,)),
            dma((2, steps, CHUNKS)),
            dma((2, steps, CHUNKS)),
            dma((RING - 1,)),
            dma((RING - 1,)),
            dma((CHUNKS, XY_COPIES)),
            dma((CHUNKS, XY_COPIES)),
            dma((3 * PIECES,)),
            dma((3 * PIECES,)),
            dma((3 * PIECES,)),
            dma((2, steps, CHUNKS)),
            dma((2, steps, CHUNKS)),
            dma((CHUNKS, XY_COPIES)),
            dma((CHUNKS, XY_COPIES)),
        ],
        compiler_params=pltpu.CompilerParams(
            collective_id=0, has_side_effects=True, vmem_limit_bytes=60 << 20
        ),
        name="layer",
    )(tokens, ids, gates, expert, w_in, w_out)


def local(tokens, gates, expert_ids, slot_expert, w_in, w_out):
    expert = slot_expert.reshape(COLS, Z // GROUP).T.reshape(-1, 1)
    return layer(tokens, expert_ids.T, gates.T, expert, w_in, w_out)


def solution(mesh):
    return jax.shard_map(
        local,
        mesh=mesh,
        in_specs=(
            P(("dp", "ep"), None),
            P(("dp", "ep"), None),
            P(("dp", "ep"), None),
            P("dp"),
            P(("dp", "ep"), None, None, None),
            P(("dp", "ep"), None, None),
        ),
        out_specs=P(("dp", "ep"), None),
        check_vma=False,
    )
```

```python
import jax
import jax.numpy as jnp
from jax import lax
from jax.experimental import pallas as pl
from jax.experimental.pallas import tpu as pltpu
from jax.sharding import PartitionSpec as P

MESH = pl.DeviceIdType.MESH
GROUP = 4
CAPE = 20
Z = 16
X = 4
Y = 2
RING = Z // 2
COLS = X * Y
WIDTHS = (512, 512, 512, 512)
CHUNKS = len(WIDTHS)
PIECES = 4
EARLY = (0, 2, 2, 2)


def z_place():
    me = lax.axis_index("ep")
    z = me % Z
    return me - z, z


def neighbours():
    base, z = z_place()
    return base + (z + 2) % Z, base + (z + Z - 2) % Z


def signal_all(devices):
    barrier = pltpu.get_barrier_semaphore()
    for device in devices:
        pl.semaphore_signal(barrier, inc=1, device_id={"ep": device}, device_id_type=MESH)
    pl.semaphore_wait(barrier, len(devices))


def columns():
    me = lax.axis_index("ep")
    return me // (X * Z), me // Z % X, me % Z


def column_at(y, x):
    return y % Y * X + x % X


def xy_peers():
    y, x, z = columns()
    return [
        column_at(y + ky, x + kx) * Z + z for ky in range(Y) for kx in range(X) if kx or ky
    ]


def xy_copies(send_ref, recv_ref, relay_ref, send_sem, recv_sem):
    y, x, z = columns()
    mine = column_at(y, x)
    half = send_ref.shape[1] // 2

    def remote(k, src, dst, column):
        return pltpu.make_async_remote_copy(
            src_ref=src,
            dst_ref=dst,
            send_sem=send_sem.at[k],
            recv_sem=recv_sem.at[k],
            device_id={"ep": column * Z + z},
            device_id_type=MESH,
        )

    relays, forwards, direct = [], [], []
    for way, step in ((0, 1), (1, X - 1)):
        rows = pl.ds(way * half, half)
        for ky in range(Y):
            k = 2 * way + ky
            slot = relay_ref.at[k]
            relays.append(
                remote(k, send_ref.at[column_at(y + ky, x + 2), rows], slot, column_at(y, x + step))
            )
            forwards.append(
                remote(
                    4 + k,
                    slot,
                    recv_ref.at[column_at(y, x + X - step), rows],
                    column_at(y + ky, x + step),
                )
            )
    for k, (ky, kx) in enumerate(((1, 1), (1, 3), (1, 0), (0, 1), (0, 3))):
        other = column_at(y + ky, x + kx)
        direct.append(remote(8 + k, send_ref.at[other], recv_ref.at[mine], other))
    return relays, forwards, direct


XY_COPIES = 13


def layer_kernel(
    tok_ref, ids_hbm, gates_hbm, expert_ref, win_ref, wout_ref, out_ref,
    held, ids_ref, gates_ref, table, meta, pick, send, recv, relay, win2, wout2, act, hidden,
    back, relay2, mix, part, come, go,
    own_sem, small_sem, zs_sem, zr_sem, ms_sem, mr_sem, xs_sem, xr_sem, ws_sem, wr_sem, wl_sem, wo_sem,
    rs_sem, rr_sem, bs_sem, br_sem,
):
    base, z = z_place()
    m, member = z // 2, z % 2
    ends = neighbours()
    rows, width = tok_ref.shape
    slots = pick.shape[1]
    half = rows // 2
    last = RING // 2 - 1
    y, x, _ = columns()
    mine = column_at(y, x)
    partner = mine * Z + z + 1 - 2 * member

    def span(chunk):
        return pl.ds(sum(WIDTHS[:chunk]), WIDTHS[chunk])

    own = []
    for chunk in range(CHUNKS):
        own.append(
            pltpu.make_async_copy(
                tok_ref.at[:, span(chunk)], held[chunk].at[pl.ds(m * rows, rows)], own_sem.at[chunk]
            )
        )
        own[-1].start()
    small = [
        pltpu.make_async_copy(ids_hbm, ids_ref, small_sem.at[0]),
        pltpu.make_async_copy(gates_hbm, gates_ref, small_sem.at[1]),
    ]
    for piece in small:
        piece.start()
    ff = win_ref.shape[2]
    mine_out = pl.ds(member * ff, ff)
    own_out = []
    for chunk in range(CHUNKS):
        own_out.append(
            pltpu.make_async_copy(
                wout_ref.at[0, :, span(chunk)], wout2[chunk].at[mine_out], wo_sem.at[chunk]
            )
        )
        own_out[-1].start()
    ring = [base + (z + 2 * k) % Z for k in range(1, RING)]
    signal_all(ring + [partner] + xy_peers())

    z_sent, started = {}, []

    def z_go(chunk, step):
        if step == 0:
            own[chunk].wait()
        for way in (0, 1):
            if step:
                z_sent[way, step - 1, chunk].wait_recv()
            owner = (m + (RING - step if way == 0 else step)) % RING
            count = half if step == last else rows
            first = way * half if step == last else 0
            there = held[chunk].at[pl.ds(owner * rows + first, count)]
            sent = pltpu.make_async_remote_copy(
                src_ref=there,
                dst_ref=there,
                send_sem=zs_sem.at[way, step, chunk],
                recv_sem=zr_sem.at[way, step, chunk],
                device_id={"ep": ends[way]},
                device_id_type=MESH,
            )
            sent.start()
            z_sent[way, step, chunk] = sent
            started.append(sent)

    queue = sorted(
        ((chunk, step) for chunk in range(CHUNKS) for step in range(last + 1)),
        key=lambda place: (2 * place[0] + place[1], place[0]),
    )
    z_go(*queue.pop(0))

    for piece in small:
        piece.wait()
    groups = Z // GROUP * COLS
    line = lax.broadcasted_iota(jnp.int32, (groups, groups), 0)
    wanted = lax.broadcasted_iota(jnp.int32, (groups, groups), 1) == (
        line % COLS * (Z // GROUP) + line // COLS
    )
    expert = jnp.sum(
        jnp.where(wanted, expert_ref[...].astype(jnp.float32), 0.0), axis=1, keepdims=True
    ).astype(jnp.int32)
    chosen = jnp.zeros((groups, rows), jnp.float32)
    gate = jnp.zeros((groups, rows), jnp.float32)
    for k in range(ids_ref.shape[0]):
        same = ids_ref[pl.ds(k, 1), :] == expert
        chosen += jnp.where(same, 1.0, 0.0)
        gate += jnp.where(same, gates_ref[pl.ds(k, 1), :], 0.0)
    earlier = lax.broadcasted_iota(jnp.int32, (rows, rows), 0) < lax.broadcasted_iota(
        jnp.int32, (rows, rows), 1
    )
    rank = jnp.dot(
        chosen.astype(jnp.bfloat16),
        jnp.where(earlier, 1.0, 0.0).astype(jnp.bfloat16),
        preferred_element_type=jnp.float32,
    )
    slot = jnp.where(chosen > 0.5, rank + (m * CAPE).astype(jnp.float32), -1.0)
    table[:, 0] = jnp.concatenate([slot, slot], axis=1).reshape(Z // GROUP, COLS, 2 * rows)
    table[:, 1] = jnp.concatenate([gate, gate], axis=1).reshape(Z // GROUP, COLS, 2 * rows)
    metas = []
    for k in range(1, RING):
        other = (m + k) % RING
        metas.append(
            pltpu.make_async_remote_copy(
                src_ref=table.at[other // 2],
                dst_ref=meta.at[m],
                send_sem=ms_sem.at[k - 1],
                recv_sem=mr_sem.at[k - 1],
                device_id={"ep": base + (z + 2 * k) % Z},
                device_id_type=MESH,
            )
        )
        metas[-1].start()
    meta[m] = table[m // 2]

    def paired(pair, kind):
        left = lax.broadcasted_iota(jnp.int32, (COLS, 2 * rows), 1) < rows
        return jnp.where(left, meta[2 * pair, kind], meta[2 * pair + 1, kind])

    def build_pick():
        for pair in range(RING // 2):
            both = paired(pair, 0)
            place = lax.broadcasted_iota(jnp.int32, (slots, 2 * rows), 0).astype(jnp.float32)
            for column in range(COLS):
                hit = place == jnp.broadcast_to(both[column : column + 1], place.shape)
                pick[column, :, pl.ds(pair * 2 * rows, 2 * rows)] = jnp.where(
                    hit, 1.0, 0.0
                ).astype(jnp.bfloat16)

    def build_mix():
        for pair in range(RING // 2):
            slot, gate = paired(pair, 0), paired(pair, 1)
            first = lax.broadcasted_iota(jnp.int32, slot.shape, 0) * slots
            slot = jnp.where(slot < 0.0, -1.0, slot + first.astype(jnp.float32)).T
            gate = gate.T
            high = gate.astype(jnp.bfloat16).astype(jnp.float32)
            low = gate - high
            for lane in range(0, COLS * slots, 128):
                place = lax.broadcasted_iota(jnp.int32, (2 * rows, 128), 1) + lane
                place = place.astype(jnp.float32)
                tops = jnp.zeros(place.shape, jnp.float32)
                rest = jnp.zeros(place.shape, jnp.float32)
                for column in range(lane // slots, (lane + 127) // slots + 1):
                    hit = place == slot[:, column : column + 1]
                    tops += jnp.where(hit, high[:, column : column + 1], 0.0)
                    rest += jnp.where(hit, low[:, column : column + 1], 0.0)
                here = pl.ds(pair * 2 * rows, 2 * rows), pl.ds(lane, 128)
                mix[0, here[0], here[1]] = tops.astype(jnp.bfloat16)
                mix[1, here[0], here[1]] = rest.astype(jnp.bfloat16)

    count = ff // PIECES
    pieces = []
    for piece in range(PIECES):
        here = pl.ds(piece * count, count)
        for side in (0, 1):
            there = pl.ds((2 * side + member) * ff + piece * count, count)
            pieces.append((win_ref.at[0, side, here], win2.at[there]))
    for chunk in range(CHUNKS):
        there = wout2[chunk].at[mine_out]
        pieces.append((there, there))
    weights, kept = [], []

    def weight_go(src, dst):
        k = len(weights)
        weights.append(
            pltpu.make_async_remote_copy(
                src_ref=src,
                dst_ref=dst,
                send_sem=ws_sem.at[k],
                recv_sem=wr_sem.at[k],
                device_id={"ep": partner},
                device_id_type=MESH,
            )
        )
        if k < 2 * PIECES:
            kept.append(pltpu.make_async_copy(src, dst, wl_sem.at[k]))
            kept[-1].start()
        else:
            own_out[k - 2 * PIECES].wait()
        weights[-1].start()

    def forward(copies):
        relays, forwards, _ = copies
        for came, sent in zip(relays, forwards):
            came.wait_recv()
            sent.start()

    exchanges = []
    for chunk in range(CHUNKS):
        while queue and 2 * queue[0][0] + queue[0][1] <= 2 * chunk + last:
            if queue[0] == (0, last):
                for sent in metas:
                    sent.wait_recv()
                build_pick()
            z_go(*queue.pop(0))
        for _ in range(EARLY[chunk] if queue else len(pieces)):
            weight_go(*pieces.pop(0))
        if chunk:
            forward(exchanges[-1])
        for way in (0, 1):
            z_sent[way, last, chunk].wait_recv()

        @pl.loop(0, COLS)
        def _(column):
            send[chunk][column] = jnp.dot(
                pick[column], held[chunk][...], preferred_element_type=jnp.float32
            ).astype(jnp.bfloat16)

        copies = xy_copies(
            send[chunk], recv[chunk], relay[chunk], xs_sem.at[chunk], xr_sem.at[chunk]
        )
        for sent in copies[0] + copies[2]:
            sent.start()
        exchanges.append(copies)
        recv[chunk][mine] = send[chunk][mine]
    build_mix()
    forward(exchanges[-1])

    tile = COLS * slots // 4
    group = COLS // 4
    for k in range(2 * PIECES):
        weights[k].wait_recv()
        kept[k].wait()
    for chunk in range(CHUNKS):
        _, forwards, direct = exchanges[chunk]
        for sent in direct + forwards:
            sent.wait_recv()

        @pl.loop(0, 4)
        def _(step):
            here = pl.ds(pl.multiple_of(step * tile, tile), tile)
            term = lax.dot_general(
                recv[chunk][pl.ds(step * group, group)].reshape(tile, WIDTHS[chunk]),
                win2[:, span(chunk)],
                (((1,), (1,)), ((), ())),
                preferred_element_type=jnp.float32,
            )
            if chunk:
                term += act[here]
            if chunk < CHUNKS - 1:
                act[here] = term
            else:
                side = hidden.shape[1]
                value = term[:, :side]
                value = value / (1.0 + jnp.exp(-value)) * term[:, side:]
                hidden[here] = value.astype(jnp.bfloat16)

    for relays, forwards, direct in exchanges:
        for sent in relays + forwards + direct:
            sent.wait_send()

    exchanges, r_sent = [], {}

    def produce(chunk):
        weights[2 * PIECES + chunk].wait_recv()

        @pl.loop(0, 4)
        def _(step):
            here = pl.ds(pl.multiple_of(step * tile, tile), tile)
            send[chunk][pl.ds(step * group, group)] = (
                jnp.dot(hidden[here], wout2[chunk][...], preferred_element_type=jnp.float32)
                .astype(jnp.bfloat16)
                .reshape(group, slots, WIDTHS[chunk])
            )

        copies = xy_copies(
            send[chunk], back[chunk], relay2[chunk], bs_sem.at[chunk], br_sem.at[chunk]
        )
        for sent in copies[0] + copies[2]:
            sent.start()
        exchanges.append(copies)
        back[chunk][mine] = send[chunk][mine]

    def merge(chunk):
        _, forwards, direct = exchanges[chunk]
        for sent in direct + forwards:
            sent.wait_recv()
        block = 256

        @pl.loop(0, RING * rows // block)
        def _(step):
            here = pl.ds(pl.multiple_of(step * block, block), block)
            values = back[chunk][...].reshape(COLS * slots, WIDTHS[chunk])
            part[chunk][here] = jnp.dot(
                mix[0, here], values, preferred_element_type=jnp.float32
            ) + jnp.dot(mix[1, here], values, preferred_element_type=jnp.float32)

    def reduce_step(chunk, step):
        for way in (0, 1):
            ahead = RING // 2 - step
            target = (m + (ahead if way == 0 else RING - ahead)) % RING
            count = half if step == 0 else rows
            first = way * half if step == 0 else 0
            value = part[chunk][pl.ds(target * rows + first, count)]
            local = pl.ds(first, count)
            if step == 0:
                go[chunk][way, step, local] = value.astype(jnp.bfloat16)
            else:
                r_sent[way, step - 1, chunk].wait_recv()
                if step == 1:
                    touched = pl.ds(way * half, half)
                    other = (1 - way) * half
                    arrived = come[chunk][way, 0, touched].astype(jnp.float32)
                    go[chunk][way, 1, touched] = (
                        value[way * half : way * half + half] + arrived
                    ).astype(jnp.bfloat16)
                    go[chunk][way, 1, pl.ds(other, half)] = value[other : other + half].astype(
                        jnp.bfloat16
                    )
                else:
                    arrived = come[chunk][way, step - 1].astype(jnp.float32)
                    go[chunk][way, step] = (value + arrived).astype(jnp.bfloat16)
            sent = pltpu.make_async_remote_copy(
                src_ref=go[chunk].at[way, step, local],
                dst_ref=come[chunk].at[way, step, local],
                send_sem=rs_sem.at[way, step, chunk],
                recv_sem=rr_sem.at[way, step, chunk],
                device_id={"ep": ends[way]},
                device_id_type=MESH,
            )
            sent.start()
            started.append(sent)
            r_sent[way, step, chunk] = sent

    def finish(chunk):
        total = part[chunk][pl.ds(m * rows, rows)]
        for way in (0, 1):
            r_sent[way, last, chunk].wait_recv()
            total += come[chunk][way, last].astype(jnp.float32)
        out_ref[:, span(chunk)] = total.astype(jnp.bfloat16)

    produce(0)
    forward(exchanges[0])
    produce(1)
    for chunk in range(CHUNKS):
        merge(chunk)
        reduce_step(chunk, 0)
        if chunk + 1 < CHUNKS:
            forward(exchanges[chunk + 1])
        if chunk + 2 < CHUNKS:
            produce(chunk + 2)
        if chunk:
            reduce_step(chunk - 1, 3)
        reduce_step(chunk, 1)
        if chunk:
            finish(chunk - 1)
        reduce_step(chunk, 2)
    reduce_step(CHUNKS - 1, 3)
    finish(CHUNKS - 1)
    for relays, forwards, direct in exchanges:
        for sent in relays + forwards + direct:
            sent.wait_send()
    for sent in started + metas + weights:
        sent.wait_send()


def layer(tokens, ids, gates, expert, w_in, w_out):
    rows, width = tokens.shape
    _, two, ff, _ = w_in.shape
    slots = RING * CAPE
    steps = RING // 2
    kind = tokens.dtype
    dma = pltpu.SemaphoreType.DMA

    def per_chunk(*lead, kind=kind):
        return [pltpu.VMEM(lead + (size,), kind) for size in WIDTHS]

    return pl.pallas_call(
        layer_kernel,
        out_shape=jax.ShapeDtypeStruct((rows, width), kind),
        in_specs=[pl.BlockSpec(memory_space=pl.ANY)] * 3
        + [pl.BlockSpec(memory_space=pltpu.VMEM)]
        + [pl.BlockSpec(memory_space=pl.ANY)] * 2,
        out_specs=pl.BlockSpec(memory_space=pltpu.VMEM),
        scratch_shapes=[
            per_chunk(RING * rows),
            pltpu.VMEM(ids.shape, ids.dtype),
            pltpu.VMEM(gates.shape, gates.dtype),
            pltpu.VMEM((Z // GROUP, 2, COLS, 2 * rows), jnp.float32),
            pltpu.VMEM((RING, 2, COLS, 2 * rows), jnp.float32),
            pltpu.VMEM((COLS, slots, RING * rows), kind),
            per_chunk(COLS, slots),
            per_chunk(COLS, slots),
            per_chunk(2 * Y, slots // 2),
            pltpu.VMEM((two * 2 * ff, width), kind),
            per_chunk(2 * ff),
            pltpu.VMEM((COLS * slots, two * 2 * ff), jnp.float32),
            pltpu.VMEM((COLS * slots, 2 * ff), kind),
            per_chunk(COLS, slots),
            per_chunk(2 * Y, slots // 2),
            pltpu.VMEM((2, RING * rows, COLS * slots), kind),
            per_chunk(RING * rows, kind=jnp.float32),
            per_chunk(2, steps, rows),
            per_chunk(2, steps, rows),
            dma((CHUNKS,)),
            dma((2,)),
            dma((2, steps, CHUNKS)),
            dma((2, steps, CHUNKS)),
            dma((RING - 1,)),
            dma((RING - 1,)),
            dma((CHUNKS, XY_COPIES)),
            dma((CHUNKS, XY_COPIES)),
            dma((2 * PIECES + CHUNKS,)),
            dma((2 * PIECES + CHUNKS,)),
            dma((2 * PIECES,)),
            dma((CHUNKS,)),
            dma((2, steps, CHUNKS)),
            dma((2, steps, CHUNKS)),
            dma((CHUNKS, XY_COPIES)),
            dma((CHUNKS, XY_COPIES)),
        ],
        compiler_params=pltpu.CompilerParams(
            collective_id=0, has_side_effects=True, vmem_limit_bytes=60 << 20
        ),
        name="layer",
    )(tokens, ids, gates, expert, w_in, w_out)


def local(tokens, gates, expert_ids, slot_expert, w_in, w_out):
    expert = slot_expert.reshape(1, -1)
    return layer(tokens, expert_ids.T, gates.T, expert, w_in, w_out)


def solution(mesh):
    return jax.shard_map(
        local,
        mesh=mesh,
        in_specs=(
            P(("dp", "ep"), None),
            P(("dp", "ep"), None),
            P(("dp", "ep"), None),
            P("dp"),
            P(("dp", "ep"), None, None, None),
            P(("dp", "ep"), None, None),
        ),
        out_specs=P(("dp", "ep"), None),
        check_vma=False,
    )
```

```python
import jax
import jax.numpy as jnp
from jax import lax
from jax.experimental import pallas as pl
from jax.experimental.pallas import tpu as pltpu
from jax.sharding import PartitionSpec as P

MESH = pl.DeviceIdType.MESH
GROUP = 4
CAPE = 20
Z = 16
X = 4
Y = 2
RING = Z // 2
COLS = X * Y
WIDTHS = (512, 512, 512, 512)
CHUNKS = len(WIDTHS)
PIECES = 4
SKEW = 1.5
EARLY = (0, 2, 2, 2)


def z_place():
    me = lax.axis_index("ep")
    z = me % Z
    return me - z, z


def neighbours():
    base, z = z_place()
    return base + (z + 2) % Z, base + (z + Z - 2) % Z


def signal_all(devices):
    barrier = pltpu.get_barrier_semaphore()
    for device in devices:
        pl.semaphore_signal(barrier, inc=1, device_id={"ep": device}, device_id_type=MESH)
    pl.semaphore_wait(barrier, len(devices))


def columns():
    me = lax.axis_index("ep")
    return me // (X * Z), me // Z % X, me % Z


def column_at(y, x):
    return y % Y * X + x % X


def xy_peers():
    y, x, z = columns()
    return [
        column_at(y + ky, x + kx) * Z + z for ky in range(Y) for kx in range(X) if kx or ky
    ]


def xy_copies(send_ref, recv_ref, relay_ref, send_sem, recv_sem):
    y, x, z = columns()
    mine = column_at(y, x)
    half = send_ref.shape[1] // 2

    def remote(k, src, dst, column):
        return pltpu.make_async_remote_copy(
            src_ref=src,
            dst_ref=dst,
            send_sem=send_sem.at[k],
            recv_sem=recv_sem.at[k],
            device_id={"ep": column * Z + z},
            device_id_type=MESH,
        )

    relays, forwards, direct = [], [], []
    for way, step in ((0, 1), (1, X - 1)):
        rows = pl.ds(way * half, half)
        for ky in range(Y):
            k = 2 * way + ky
            slot = relay_ref.at[k]
            relays.append(
                remote(k, send_ref.at[column_at(y + ky, x + 2), rows], slot, column_at(y, x + step))
            )
            forwards.append(
                remote(
                    4 + k,
                    slot,
                    recv_ref.at[column_at(y, x + X - step), rows],
                    column_at(y + ky, x + step),
                )
            )
    for k, (ky, kx) in enumerate(((1, 1), (1, 3), (1, 0), (0, 1), (0, 3))):
        other = column_at(y + ky, x + kx)
        direct.append(remote(8 + k, send_ref.at[other], recv_ref.at[mine], other))
    return relays, forwards, direct


XY_COPIES = 13


def layer_kernel(
    tok_ref, ids_hbm, gates_hbm, expert_ref, win_ref, wout_ref, out_ref,
    held, ids_ref, gates_ref, table, meta, pick, send, recv, relay, win2, wout2, act, hidden,
    back, relay2, mix, part, come, go,
    own_sem, small_sem, zs_sem, zr_sem, ms_sem, mr_sem, xs_sem, xr_sem, ws_sem, wr_sem, wl_sem, wo_sem,
    rs_sem, rr_sem, bs_sem, br_sem,
):
    base, z = z_place()
    m, member = z // 2, z % 2
    ends = neighbours()
    rows, width = tok_ref.shape
    slots = pick.shape[1]
    half = rows // 2
    last = RING // 2 - 1
    y, x, _ = columns()
    mine = column_at(y, x)
    partner = mine * Z + z + 1 - 2 * member

    def span(chunk):
        return pl.ds(sum(WIDTHS[:chunk]), WIDTHS[chunk])

    own = []
    for chunk in range(CHUNKS):
        own.append(
            pltpu.make_async_copy(
                tok_ref.at[:, span(chunk)], held[chunk].at[pl.ds(m * rows, rows)], own_sem.at[chunk]
            )
        )
        own[-1].start()
    small = [
        pltpu.make_async_copy(ids_hbm, ids_ref, small_sem.at[0]),
        pltpu.make_async_copy(gates_hbm, gates_ref, small_sem.at[1]),
    ]
    for piece in small:
        piece.start()
    ff = win_ref.shape[2]
    mine_out = pl.ds(member * ff, ff)
    own_out = []
    for chunk in range(CHUNKS):
        own_out.append(
            pltpu.make_async_copy(
                wout_ref.at[0, :, span(chunk)], wout2[chunk].at[mine_out], wo_sem.at[chunk]
            )
        )
        own_out[-1].start()
    ring = [base + (z + 2 * k) % Z for k in range(1, RING)]
    signal_all(ring + [partner] + xy_peers())

    z_sent, started = {}, []

    def z_go(chunk, step):
        if step == 0:
            own[chunk].wait()
        for part_of in (0, 1):
            for way in (0, 1):
                if step == last and way != part_of:
                    continue
                if step:
                    z_sent[way, step - 1, chunk, part_of].wait_recv()
                owner = (m + (RING - step if way == 0 else step)) % RING
                there = held[chunk].at[pl.ds(owner * rows + part_of * half, half)]
                sent = pltpu.make_async_remote_copy(
                    src_ref=there,
                    dst_ref=there,
                    send_sem=zs_sem.at[way, step, chunk, part_of],
                    recv_sem=zr_sem.at[way, step, chunk, part_of],
                    device_id={"ep": ends[way]},
                    device_id_type=MESH,
                )
                sent.start()
                z_sent[way, step, chunk, part_of] = sent
                started.append(sent)

    queue = sorted(
        ((chunk, step) for chunk in range(CHUNKS) for step in range(last + 1)),
        key=lambda place: (SKEW * place[0] + place[1], place[0]),
    )
    z_go(*queue.pop(0))

    for piece in small:
        piece.wait()
    groups = Z // GROUP * COLS
    line = lax.broadcasted_iota(jnp.int32, (groups, groups), 0)
    wanted = lax.broadcasted_iota(jnp.int32, (groups, groups), 1) == (
        line % COLS * (Z // GROUP) + line // COLS
    )
    expert = jnp.sum(
        jnp.where(wanted, expert_ref[...].astype(jnp.float32), 0.0), axis=1, keepdims=True
    ).astype(jnp.int32)
    chosen = jnp.zeros((groups, rows), jnp.float32)
    gate = jnp.zeros((groups, rows), jnp.float32)
    for k in range(ids_ref.shape[0]):
        same = ids_ref[pl.ds(k, 1), :] == expert
        chosen += jnp.where(same, 1.0, 0.0)
        gate += jnp.where(same, gates_ref[pl.ds(k, 1), :], 0.0)
    earlier = lax.broadcasted_iota(jnp.int32, (rows, rows), 0) < lax.broadcasted_iota(
        jnp.int32, (rows, rows), 1
    )
    rank = jnp.dot(
        chosen.astype(jnp.bfloat16),
        jnp.where(earlier, 1.0, 0.0).astype(jnp.bfloat16),
        preferred_element_type=jnp.float32,
    )
    slot = jnp.where(chosen > 0.5, rank + (m * CAPE).astype(jnp.float32), -1.0)
    table[:, 0] = jnp.concatenate([slot, slot], axis=1).reshape(Z // GROUP, COLS, 2 * rows)
    table[:, 1] = jnp.concatenate([gate, gate], axis=1).reshape(Z // GROUP, COLS, 2 * rows)
    metas = []
    for k in range(1, RING):
        other = (m + k) % RING
        metas.append(
            pltpu.make_async_remote_copy(
                src_ref=table.at[other // 2],
                dst_ref=meta.at[m],
                send_sem=ms_sem.at[k - 1],
                recv_sem=mr_sem.at[k - 1],
                device_id={"ep": base + (z + 2 * k) % Z},
                device_id_type=MESH,
            )
        )
        metas[-1].start()
    meta[m] = table[m // 2]

    def paired(pair, kind):
        left = lax.broadcasted_iota(jnp.int32, (COLS, 2 * rows), 1) < rows
        return jnp.where(left, meta[2 * pair, kind], meta[2 * pair + 1, kind])

    def build_pick():
        for pair in range(RING // 2):
            both = paired(pair, 0)
            place = lax.broadcasted_iota(jnp.int32, (slots, 2 * rows), 0).astype(jnp.float32)
            for column in range(COLS):
                hit = place == jnp.broadcast_to(both[column : column + 1], place.shape)
                pick[column, :, pl.ds(pair * 2 * rows, 2 * rows)] = jnp.where(
                    hit, 1.0, 0.0
                ).astype(jnp.bfloat16)

    def build_mix():
        for pair in range(RING // 2):
            slot, gate = paired(pair, 0), paired(pair, 1)
            first = lax.broadcasted_iota(jnp.int32, slot.shape, 0) * slots
            slot = jnp.where(slot < 0.0, -1.0, slot + first.astype(jnp.float32)).T
            gate = gate.T
            high = gate.astype(jnp.bfloat16).astype(jnp.float32)
            low = gate - high
            for lane in range(0, COLS * slots, 128):
                place = lax.broadcasted_iota(jnp.int32, (2 * rows, 128), 1) + lane
                place = place.astype(jnp.float32)
                tops = jnp.zeros(place.shape, jnp.float32)
                rest = jnp.zeros(place.shape, jnp.float32)
                for column in range(lane // slots, (lane + 127) // slots + 1):
                    hit = place == slot[:, column : column + 1]
                    tops += jnp.where(hit, high[:, column : column + 1], 0.0)
                    rest += jnp.where(hit, low[:, column : column + 1], 0.0)
                here = pl.ds(pair * 2 * rows, 2 * rows), pl.ds(lane, 128)
                mix[0, here[0], here[1]] = tops.astype(jnp.bfloat16)
                mix[1, here[0], here[1]] = rest.astype(jnp.bfloat16)

    count = ff // PIECES
    pieces = []
    for piece in range(PIECES):
        here = pl.ds(piece * count, count)
        for side in (0, 1):
            there = pl.ds((2 * side + member) * ff + piece * count, count)
            pieces.append((win_ref.at[0, side, here], win2.at[there]))
    for chunk in range(CHUNKS):
        there = wout2[chunk].at[mine_out]
        pieces.append((there, there))
    weights, kept = [], []

    def weight_go(src, dst):
        k = len(weights)
        weights.append(
            pltpu.make_async_remote_copy(
                src_ref=src,
                dst_ref=dst,
                send_sem=ws_sem.at[k],
                recv_sem=wr_sem.at[k],
                device_id={"ep": partner},
                device_id_type=MESH,
            )
        )
        if k < 2 * PIECES:
            kept.append(pltpu.make_async_copy(src, dst, wl_sem.at[k]))
            kept[-1].start()
        else:
            own_out[k - 2 * PIECES].wait()
        weights[-1].start()

    def forward(copies):
        relays, forwards, _ = copies
        for came, sent in zip(relays, forwards):
            came.wait_recv()
            sent.start()

    exchanges = []
    for chunk in range(CHUNKS):
        while queue and SKEW * queue[0][0] + queue[0][1] <= SKEW * chunk + last:
            if queue[0] == (0, last):
                for sent in metas:
                    sent.wait_recv()
                build_pick()
            z_go(*queue.pop(0))
        for _ in range(EARLY[chunk] if queue else len(pieces)):
            weight_go(*pieces.pop(0))
        if chunk:
            forward(exchanges[-1])
        for way in (0, 1):
            z_sent[way, last - 1, chunk, 1 - way].wait_recv()
            z_sent[way, last, chunk, way].wait_recv()

        @pl.loop(0, COLS)
        def _(column):
            send[chunk][column] = jnp.dot(
                pick[column], held[chunk][...], preferred_element_type=jnp.float32
            ).astype(jnp.bfloat16)

        copies = xy_copies(
            send[chunk], recv[chunk], relay[chunk], xs_sem.at[chunk], xr_sem.at[chunk]
        )
        for sent in copies[0] + copies[2]:
            sent.start()
        exchanges.append(copies)
        recv[chunk][mine] = send[chunk][mine]
    build_mix()
    forward(exchanges[-1])

    tile = COLS * slots // 4
    group = COLS // 4
    for k in range(2 * PIECES):
        weights[k].wait_recv()
        kept[k].wait()
    for chunk in range(CHUNKS):
        _, forwards, direct = exchanges[chunk]
        for sent in direct + forwards:
            sent.wait_recv()

        @pl.loop(0, 4)
        def _(step):
            here = pl.ds(pl.multiple_of(step * tile, tile), tile)
            term = lax.dot_general(
                recv[chunk][pl.ds(step * group, group)].reshape(tile, WIDTHS[chunk]),
                win2[:, span(chunk)],
                (((1,), (1,)), ((), ())),
                preferred_element_type=jnp.float32,
            )
            if chunk:
                term += act[here]
            if chunk < CHUNKS - 1:
                act[here] = term
            else:
                side = hidden.shape[1]
                value = term[:, :side]
                value = value / (1.0 + jnp.exp(-value)) * term[:, side:]
                hidden[here] = value.astype(jnp.bfloat16)

    for relays, forwards, direct in exchanges:
        for sent in relays + forwards + direct:
            sent.wait_send()

    exchanges, r_sent = [], {}

    def produce(chunk):
        weights[2 * PIECES + chunk].wait_recv()

        @pl.loop(0, 4)
        def _(step):
            here = pl.ds(pl.multiple_of(step * tile, tile), tile)
            send[chunk][pl.ds(step * group, group)] = (
                jnp.dot(hidden[here], wout2[chunk][...], preferred_element_type=jnp.float32)
                .astype(jnp.bfloat16)
                .reshape(group, slots, WIDTHS[chunk])
            )

        copies = xy_copies(
            send[chunk], back[chunk], relay2[chunk], bs_sem.at[chunk], br_sem.at[chunk]
        )
        for sent in copies[0] + copies[2]:
            sent.start()
        exchanges.append(copies)
        back[chunk][mine] = send[chunk][mine]

    def merge(chunk):
        _, forwards, direct = exchanges[chunk]
        for sent in direct + forwards:
            sent.wait_recv()
        block = 256

        @pl.loop(0, RING * rows // block)
        def _(step):
            here = pl.ds(pl.multiple_of(step * block, block), block)
            values = back[chunk][...].reshape(COLS * slots, WIDTHS[chunk])
            part[chunk][here] = jnp.dot(
                mix[0, here], values, preferred_element_type=jnp.float32
            ) + jnp.dot(mix[1, here], values, preferred_element_type=jnp.float32)

    def reduce_step(chunk, step):
        for part_of in (0, 1):
            local = pl.ds(part_of * half, half)
            for way in (0, 1):
                if step == 0 and way != part_of:
                    continue
                ahead = RING // 2 - step
                target = (m + (ahead if way == 0 else RING - ahead)) % RING
                value = part[chunk][pl.ds(target * rows + part_of * half, half)]
                before = r_sent.get((way, step - 1, chunk, part_of))
                if before is not None:
                    before.wait_recv()
                    value += come[chunk][way, step - 1, local].astype(jnp.float32)
                go[chunk][way, step, local] = value.astype(jnp.bfloat16)
                sent = pltpu.make_async_remote_copy(
                    src_ref=go[chunk].at[way, step, local],
                    dst_ref=come[chunk].at[way, step, local],
                    send_sem=rs_sem.at[way, step, chunk, part_of],
                    recv_sem=rr_sem.at[way, step, chunk, part_of],
                    device_id={"ep": ends[way]},
                    device_id_type=MESH,
                )
                sent.start()
                started.append(sent)
                r_sent[way, step, chunk, part_of] = sent

    def finish(chunk):
        total = part[chunk][pl.ds(m * rows, rows)]
        for way in (0, 1):
            for part_of in (0, 1):
                r_sent[way, last, chunk, part_of].wait_recv()
            total += come[chunk][way, last].astype(jnp.float32)
        out_ref[:, span(chunk)] = total.astype(jnp.bfloat16)

    produce(0)
    forward(exchanges[0])
    produce(1)
    for chunk in range(CHUNKS):
        merge(chunk)
        reduce_step(chunk, 0)
        if chunk:
            reduce_step(chunk - 1, 2)
        if chunk + 1 < CHUNKS:
            forward(exchanges[chunk + 1])
        if chunk + 2 < CHUNKS:
            produce(chunk + 2)
        reduce_step(chunk, 1)
        if chunk:
            reduce_step(chunk - 1, 3)
        if chunk > 1:
            finish(chunk - 2)
    reduce_step(CHUNKS - 1, 2)
    finish(CHUNKS - 2)
    reduce_step(CHUNKS - 1, 3)
    finish(CHUNKS - 1)
    for relays, forwards, direct in exchanges:
        for sent in relays + forwards + direct:
            sent.wait_send()
    for sent in started + metas + weights:
        sent.wait_send()


def layer(tokens, ids, gates, expert, w_in, w_out):
    rows, width = tokens.shape
    _, two, ff, _ = w_in.shape
    slots = RING * CAPE
    steps = RING // 2
    kind = tokens.dtype
    dma = pltpu.SemaphoreType.DMA

    def per_chunk(*lead, kind=kind):
        return [pltpu.VMEM(lead + (size,), kind) for size in WIDTHS]

    return pl.pallas_call(
        layer_kernel,
        out_shape=jax.ShapeDtypeStruct((rows, width), kind),
        in_specs=[pl.BlockSpec(memory_space=pl.ANY)] * 3
        + [pl.BlockSpec(memory_space=pltpu.VMEM)]
        + [pl.BlockSpec(memory_space=pl.ANY)] * 2,
        out_specs=pl.BlockSpec(memory_space=pltpu.VMEM),
        scratch_shapes=[
            per_chunk(RING * rows),
            pltpu.VMEM(ids.shape, ids.dtype),
            pltpu.VMEM(gates.shape, gates.dtype),
            pltpu.VMEM((Z // GROUP, 2, COLS, 2 * rows), jnp.float32),
            pltpu.VMEM((RING, 2, COLS, 2 * rows), jnp.float32),
            pltpu.VMEM((COLS, slots, RING * rows), kind),
            per_chunk(COLS, slots),
            per_chunk(COLS, slots),
            per_chunk(2 * Y, slots // 2),
            pltpu.VMEM((two * 2 * ff, width), kind),
            per_chunk(2 * ff),
            pltpu.VMEM((COLS * slots, two * 2 * ff), jnp.float32),
            pltpu.VMEM((COLS * slots, 2 * ff), kind),
            per_chunk(COLS, slots),
            per_chunk(2 * Y, slots // 2),
            pltpu.VMEM((2, RING * rows, COLS * slots), kind),
            per_chunk(RING * rows, kind=jnp.float32),
            per_chunk(2, steps, rows),
            per_chunk(2, steps, rows),
            dma((CHUNKS,)),
            dma((2,)),
            dma((2, steps, CHUNKS, 2)),
            dma((2, steps, CHUNKS, 2)),
            dma((RING - 1,)),
            dma((RING - 1,)),
            dma((CHUNKS, XY_COPIES)),
            dma((CHUNKS, XY_COPIES)),
            dma((2 * PIECES + CHUNKS,)),
            dma((2 * PIECES + CHUNKS,)),
            dma((2 * PIECES,)),
            dma((CHUNKS,)),
            dma((2, steps, CHUNKS, 2)),
            dma((2, steps, CHUNKS, 2)),
            dma((CHUNKS, XY_COPIES)),
            dma((CHUNKS, XY_COPIES)),
        ],
        compiler_params=pltpu.CompilerParams(
            collective_id=0, has_side_effects=True, vmem_limit_bytes=60 << 20
        ),
        name="layer",
    )(tokens, ids, gates, expert, w_in, w_out)


def local(tokens, gates, expert_ids, slot_expert, w_in, w_out):
    expert = slot_expert.reshape(1, -1)
    return layer(tokens, expert_ids.T, gates.T, expert, w_in, w_out)


def solution(mesh):
    return jax.shard_map(
        local,
        mesh=mesh,
        in_specs=(
            P(("dp", "ep"), None),
            P(("dp", "ep"), None),
            P(("dp", "ep"), None),
            P("dp"),
            P(("dp", "ep"), None, None, None),
            P(("dp", "ep"), None, None),
        ),
        out_specs=P(("dp", "ep"), None),
        check_vma=False,
    )
```

```python
import jax
import jax.numpy as jnp
from jax import lax
from jax.experimental import pallas as pl
from jax.experimental.pallas import tpu as pltpu
from jax.sharding import PartitionSpec as P

MESH = pl.DeviceIdType.MESH
GROUP = 4
CAPE = 20
Z = 16
X = 4
Y = 2
RING = Z // 2
COLS = X * Y
WIDTHS = (512, 512, 512, 512)
CHUNKS = len(WIDTHS)
PIECES = 4
SKEW = 1
EARLY = (1, 1, 2, 2)


def z_place():
    me = lax.axis_index("ep")
    z = me % Z
    return me - z, z


def neighbours():
    base, z = z_place()
    return base + (z + 2) % Z, base + (z + Z - 2) % Z


def signal_all(devices):
    barrier = pltpu.get_barrier_semaphore()
    for device in devices:
        pl.semaphore_signal(barrier, inc=1, device_id={"ep": device}, device_id_type=MESH)
    pl.semaphore_wait(barrier, len(devices))


def columns():
    me = lax.axis_index("ep")
    return me // (X * Z), me // Z % X, me % Z


def column_at(y, x):
    return y % Y * X + x % X


def xy_peers():
    y, x, z = columns()
    return [
        column_at(y + ky, x + kx) * Z + z for ky in range(Y) for kx in range(X) if kx or ky
    ]


def xy_copies(send_ref, recv_ref, relay_ref, send_sem, recv_sem):
    y, x, z = columns()
    mine = column_at(y, x)
    half = send_ref.shape[1] // 2

    def remote(k, src, dst, column):
        return pltpu.make_async_remote_copy(
            src_ref=src,
            dst_ref=dst,
            send_sem=send_sem.at[k],
            recv_sem=recv_sem.at[k],
            device_id={"ep": column * Z + z},
            device_id_type=MESH,
        )

    relays, forwards, direct = [], [], []
    for way, step in ((0, 1), (1, X - 1)):
        rows = pl.ds(way * half, half)
        for ky in range(Y):
            k = 2 * way + ky
            slot = relay_ref.at[k]
            relays.append(
                remote(k, send_ref.at[column_at(y + ky, x + 2), rows], slot, column_at(y, x + step))
            )
            forwards.append(
                remote(
                    4 + k,
                    slot,
                    recv_ref.at[column_at(y, x + X - step), rows],
                    column_at(y + ky, x + step),
                )
            )
    for k, (ky, kx) in enumerate(((1, 1), (1, 3), (1, 0), (0, 1), (0, 3))):
        other = column_at(y + ky, x + kx)
        direct.append(remote(8 + k, send_ref.at[other], recv_ref.at[mine], other))
    return relays, forwards, direct


XY_COPIES = 13


def layer_kernel(
    tok_ref, ids_hbm, gates_hbm, expert_ref, win_ref, wout_ref, out_ref,
    held, ids_ref, gates_ref, table, meta, pick, send, recv, relay, win2, wout2, act, hidden,
    back, relay2, mix, part, come, go,
    own_sem, small_sem, zs_sem, zr_sem, ms_sem, mr_sem, xs_sem, xr_sem, ws_sem, wr_sem, wl_sem, wo_sem,
    rs_sem, rr_sem, bs_sem, br_sem,
):
    base, z = z_place()
    m, member = z // 2, z % 2
    ends = neighbours()
    rows, width = tok_ref.shape
    slots = pick.shape[1]
    half = rows // 2
    last = RING // 2 - 1
    y, x, _ = columns()
    mine = column_at(y, x)
    partner = mine * Z + z + 1 - 2 * member

    def span(chunk):
        return pl.ds(sum(WIDTHS[:chunk]), WIDTHS[chunk])

    own = []
    for chunk in range(CHUNKS):
        own.append(
            pltpu.make_async_copy(
                tok_ref.at[:, span(chunk)], held[chunk].at[pl.ds(m * rows, rows)], own_sem.at[chunk]
            )
        )
        own[-1].start()
    small = [
        pltpu.make_async_copy(ids_hbm, ids_ref, small_sem.at[0]),
        pltpu.make_async_copy(gates_hbm, gates_ref, small_sem.at[1]),
    ]
    for piece in small:
        piece.start()
    ff = win_ref.shape[2]
    mine_out = pl.ds(member * ff, ff)
    own_out = []
    for chunk in range(CHUNKS):
        own_out.append(
            pltpu.make_async_copy(
                wout_ref.at[0, :, span(chunk)], wout2[chunk].at[mine_out], wo_sem.at[chunk]
            )
        )
        own_out[-1].start()
    ring = [base + (z + 2 * k) % Z for k in range(1, RING)]
    signal_all(ring + [partner] + xy_peers())

    z_sent, started = {}, []

    def z_go(chunk, step):
        if step == 0:
            own[chunk].wait()
        for part_of in (0, 1):
            for way in (0, 1):
                if step == last and way != part_of:
                    continue
                if step:
                    z_sent[way, step - 1, chunk, part_of].wait_recv()
                owner = (m + (RING - step if way == 0 else step)) % RING
                there = held[chunk].at[pl.ds(owner * rows + part_of * half, half)]
                sent = pltpu.make_async_remote_copy(
                    src_ref=there,
                    dst_ref=there,
                    send_sem=zs_sem.at[way, step, chunk, part_of],
                    recv_sem=zr_sem.at[way, step, chunk, part_of],
                    device_id={"ep": ends[way]},
                    device_id_type=MESH,
                )
                sent.start()
                z_sent[way, step, chunk, part_of] = sent
                started.append(sent)

    queue = sorted(
        ((chunk, step) for chunk in range(CHUNKS) for step in range(last + 1)),
        key=lambda place: (SKEW * place[0] + place[1], place[0]),
    )
    z_go(*queue.pop(0))

    for piece in small:
        piece.wait()
    groups = Z // GROUP * COLS
    line = lax.broadcasted_iota(jnp.int32, (groups, groups), 0)
    wanted = lax.broadcasted_iota(jnp.int32, (groups, groups), 1) == (
        line % COLS * (Z // GROUP) + line // COLS
    )
    expert = jnp.sum(
        jnp.where(wanted, expert_ref[...].astype(jnp.float32), 0.0), axis=1, keepdims=True
    ).astype(jnp.int32)
    chosen = jnp.zeros((groups, rows), jnp.float32)
    gate = jnp.zeros((groups, rows), jnp.float32)
    for k in range(ids_ref.shape[0]):
        same = ids_ref[pl.ds(k, 1), :] == expert
        chosen += jnp.where(same, 1.0, 0.0)
        gate += jnp.where(same, gates_ref[pl.ds(k, 1), :], 0.0)
    earlier = lax.broadcasted_iota(jnp.int32, (rows, rows), 0) < lax.broadcasted_iota(
        jnp.int32, (rows, rows), 1
    )
    rank = jnp.dot(
        chosen.astype(jnp.bfloat16),
        jnp.where(earlier, 1.0, 0.0).astype(jnp.bfloat16),
        preferred_element_type=jnp.float32,
    )
    slot = jnp.where(chosen > 0.5, rank + (m * CAPE).astype(jnp.float32), -1.0)
    table[:, 0] = jnp.concatenate([slot, slot], axis=1).reshape(Z // GROUP, COLS, 2 * rows)
    table[:, 1] = jnp.concatenate([gate, gate], axis=1).reshape(Z // GROUP, COLS, 2 * rows)
    metas = []
    for k in range(1, RING):
        other = (m + k) % RING
        metas.append(
            pltpu.make_async_remote_copy(
                src_ref=table.at[other // 2],
                dst_ref=meta.at[m],
                send_sem=ms_sem.at[k - 1],
                recv_sem=mr_sem.at[k - 1],
                device_id={"ep": base + (z + 2 * k) % Z},
                device_id_type=MESH,
            )
        )
        metas[-1].start()
    meta[m] = table[m // 2]

    def paired(pair, kind):
        left = lax.broadcasted_iota(jnp.int32, (COLS, 2 * rows), 1) < rows
        return jnp.where(left, meta[2 * pair, kind], meta[2 * pair + 1, kind])

    def build_pick():
        for pair in range(RING // 2):
            both = paired(pair, 0)
            place = lax.broadcasted_iota(jnp.int32, (slots, 2 * rows), 0).astype(jnp.float32)
            for column in range(COLS):
                hit = place == jnp.broadcast_to(both[column : column + 1], place.shape)
                pick[column, :, pl.ds(pair * 2 * rows, 2 * rows)] = jnp.where(
                    hit, 1.0, 0.0
                ).astype(jnp.bfloat16)

    def build_mix():
        for pair in range(RING // 2):
            slot, gate = paired(pair, 0), paired(pair, 1)
            first = lax.broadcasted_iota(jnp.int32, slot.shape, 0) * slots
            slot = jnp.where(slot < 0.0, -1.0, slot + first.astype(jnp.float32)).T
            gate = gate.T
            high = gate.astype(jnp.bfloat16).astype(jnp.float32)
            low = gate - high
            for lane in range(0, COLS * slots, 128):
                place = lax.broadcasted_iota(jnp.int32, (2 * rows, 128), 1) + lane
                place = place.astype(jnp.float32)
                tops = jnp.zeros(place.shape, jnp.float32)
                rest = jnp.zeros(place.shape, jnp.float32)
                for column in range(lane // slots, (lane + 127) // slots + 1):
                    hit = place == slot[:, column : column + 1]
                    tops += jnp.where(hit, high[:, column : column + 1], 0.0)
                    rest += jnp.where(hit, low[:, column : column + 1], 0.0)
                here = pl.ds(pair * 2 * rows, 2 * rows), pl.ds(lane, 128)
                mix[0, here[0], here[1]] = tops.astype(jnp.bfloat16)
                mix[1, here[0], here[1]] = rest.astype(jnp.bfloat16)

    count = ff // PIECES
    pieces = []
    for piece in range(PIECES):
        here = pl.ds(piece * count, count)
        for side in (0, 1):
            there = pl.ds((2 * side + member) * ff + piece * count, count)
            pieces.append((win_ref.at[0, side, here], win2.at[there]))
    for chunk in range(CHUNKS):
        there = wout2[chunk].at[mine_out]
        pieces.append((there, there))
    weights, kept = [], []

    def weight_go(src, dst):
        k = len(weights)
        weights.append(
            pltpu.make_async_remote_copy(
                src_ref=src,
                dst_ref=dst,
                send_sem=ws_sem.at[k],
                recv_sem=wr_sem.at[k],
                device_id={"ep": partner},
                device_id_type=MESH,
            )
        )
        if k < 2 * PIECES:
            kept.append(pltpu.make_async_copy(src, dst, wl_sem.at[k]))
            kept[-1].start()
        else:
            own_out[k - 2 * PIECES].wait()
        weights[-1].start()

    def forward(copies):
        relays, forwards, _ = copies
        for came, sent in zip(relays, forwards):
            came.wait_recv()
            sent.start()

    exchanges = []
    for chunk in range(CHUNKS):
        while queue and SKEW * queue[0][0] + queue[0][1] <= SKEW * chunk + last:
            if queue[0] == (0, last):
                for sent in metas:
                    sent.wait_recv()
                build_pick()
            z_go(*queue.pop(0))
        for _ in range(EARLY[chunk] if queue else len(pieces)):
            weight_go(*pieces.pop(0))
        if chunk:
            forward(exchanges[-1])
        for way in (0, 1):
            z_sent[way, last - 1, chunk, 1 - way].wait_recv()
            z_sent[way, last, chunk, way].wait_recv()

        @pl.loop(0, COLS)
        def _(column):
            send[chunk][column] = jnp.dot(
                pick[column], held[chunk][...], preferred_element_type=jnp.float32
            ).astype(jnp.bfloat16)

        copies = xy_copies(
            send[chunk], recv[chunk], relay[chunk], xs_sem.at[chunk], xr_sem.at[chunk]
        )
        for sent in copies[0] + copies[2]:
            sent.start()
        exchanges.append(copies)
        recv[chunk][mine] = send[chunk][mine]
    build_mix()
    forward(exchanges[-1])

    tile = COLS * slots // 4
    group = COLS // 4
    for k in range(2 * PIECES):
        weights[k].wait_recv()
        kept[k].wait()
    for chunk in range(CHUNKS):
        _, forwards, direct = exchanges[chunk]
        for sent in direct + forwards:
            sent.wait_recv()

        @pl.loop(0, 4)
        def _(step):
            here = pl.ds(pl.multiple_of(step * tile, tile), tile)
            term = lax.dot_general(
                recv[chunk][pl.ds(step * group, group)].reshape(tile, WIDTHS[chunk]),
                win2[:, span(chunk)],
                (((1,), (1,)), ((), ())),
                preferred_element_type=jnp.float32,
            )
            if chunk:
                term += act[here]
            if chunk < CHUNKS - 1:
                act[here] = term
            else:
                side = hidden.shape[1]
                value = term[:, :side]
                value = value / (1.0 + jnp.exp(-value)) * term[:, side:]
                hidden[here] = value.astype(jnp.bfloat16)

    for relays, forwards, direct in exchanges:
        for sent in relays + forwards + direct:
            sent.wait_send()

    exchanges, r_sent = [], {}

    def produce(chunk):
        weights[2 * PIECES + chunk].wait_recv()

        @pl.loop(0, 4)
        def _(step):
            here = pl.ds(pl.multiple_of(step * tile, tile), tile)
            send[chunk][pl.ds(step * group, group)] = (
                jnp.dot(hidden[here], wout2[chunk][...], preferred_element_type=jnp.float32)
                .astype(jnp.bfloat16)
                .reshape(group, slots, WIDTHS[chunk])
            )

        copies = xy_copies(
            send[chunk], back[chunk], relay2[chunk], bs_sem.at[chunk], br_sem.at[chunk]
        )
        for sent in copies[0] + copies[2]:
            sent.start()
        exchanges.append(copies)
        back[chunk][mine] = send[chunk][mine]

    def merge(chunk):
        _, forwards, direct = exchanges[chunk]
        for sent in direct + forwards:
            sent.wait_recv()
        block = 256

        @pl.loop(0, RING * rows // block)
        def _(step):
            here = pl.ds(pl.multiple_of(step * block, block), block)
            values = back[chunk][...].reshape(COLS * slots, WIDTHS[chunk])
            part[chunk][here] = jnp.dot(
                mix[0, here], values, preferred_element_type=jnp.float32
            ) + jnp.dot(mix[1, here], values, preferred_element_type=jnp.float32)

    def reduce_step(chunk, step):
        for part_of in (0, 1):
            local = pl.ds(part_of * half, half)
            for way in (0, 1):
                if step == 0 and way != part_of:
                    continue
                ahead = RING // 2 - step
                target = (m + (ahead if way == 0 else RING - ahead)) % RING
                value = part[chunk][pl.ds(target * rows + part_of * half, half)]
                before = r_sent.get((way, step - 1, chunk, part_of))
                if before is not None:
                    before.wait_recv()
                    value += come[chunk][way, step - 1, local].astype(jnp.float32)
                go[chunk][way, step, local] = value.astype(jnp.bfloat16)
                sent = pltpu.make_async_remote_copy(
                    src_ref=go[chunk].at[way, step, local],
                    dst_ref=come[chunk].at[way, step, local],
                    send_sem=rs_sem.at[way, step, chunk, part_of],
                    recv_sem=rr_sem.at[way, step, chunk, part_of],
                    device_id={"ep": ends[way]},
                    device_id_type=MESH,
                )
                sent.start()
                started.append(sent)
                r_sent[way, step, chunk, part_of] = sent

    def finish(chunk):
        total = part[chunk][pl.ds(m * rows, rows)]
        for way in (0, 1):
            for part_of in (0, 1):
                r_sent[way, last, chunk, part_of].wait_recv()
            total += come[chunk][way, last].astype(jnp.float32)
        out_ref[:, span(chunk)] = total.astype(jnp.bfloat16)

    produce(0)
    forward(exchanges[0])
    produce(1)
    for chunk in range(CHUNKS):
        merge(chunk)
        reduce_step(chunk, 0)
        if chunk:
            reduce_step(chunk - 1, 2)
        if chunk + 1 < CHUNKS:
            forward(exchanges[chunk + 1])
        if chunk + 2 < CHUNKS:
            produce(chunk + 2)
        reduce_step(chunk, 1)
        if chunk:
            reduce_step(chunk - 1, 3)
        if chunk > 1:
            finish(chunk - 2)
    reduce_step(CHUNKS - 1, 2)
    finish(CHUNKS - 2)
    reduce_step(CHUNKS - 1, 3)
    finish(CHUNKS - 1)
    for relays, forwards, direct in exchanges:
        for sent in relays + forwards + direct:
            sent.wait_send()
    for sent in started + metas + weights:
        sent.wait_send()


def layer(tokens, ids, gates, expert, w_in, w_out):
    rows, width = tokens.shape
    _, two, ff, _ = w_in.shape
    slots = RING * CAPE
    steps = RING // 2
    kind = tokens.dtype
    dma = pltpu.SemaphoreType.DMA

    def per_chunk(*lead, kind=kind):
        return [pltpu.VMEM(lead + (size,), kind) for size in WIDTHS]

    return pl.pallas_call(
        layer_kernel,
        out_shape=jax.ShapeDtypeStruct((rows, width), kind),
        in_specs=[pl.BlockSpec(memory_space=pl.ANY)] * 3
        + [pl.BlockSpec(memory_space=pltpu.VMEM)]
        + [pl.BlockSpec(memory_space=pl.ANY)] * 2,
        out_specs=pl.BlockSpec(memory_space=pltpu.VMEM),
        scratch_shapes=[
            per_chunk(RING * rows),
            pltpu.VMEM(ids.shape, ids.dtype),
            pltpu.VMEM(gates.shape, gates.dtype),
            pltpu.VMEM((Z // GROUP, 2, COLS, 2 * rows), jnp.float32),
            pltpu.VMEM((RING, 2, COLS, 2 * rows), jnp.float32),
            pltpu.VMEM((COLS, slots, RING * rows), kind),
            per_chunk(COLS, slots),
            per_chunk(COLS, slots),
            per_chunk(2 * Y, slots // 2),
            pltpu.VMEM((two * 2 * ff, width), kind),
            per_chunk(2 * ff),
            pltpu.VMEM((COLS * slots, two * 2 * ff), jnp.float32),
            pltpu.VMEM((COLS * slots, 2 * ff), kind),
            per_chunk(COLS, slots),
            per_chunk(2 * Y, slots // 2),
            pltpu.VMEM((2, RING * rows, COLS * slots), kind),
            per_chunk(RING * rows, kind=jnp.float32),
            per_chunk(2, steps, rows),
            per_chunk(2, steps, rows),
            dma((CHUNKS,)),
            dma((2,)),
            dma((2, steps, CHUNKS, 2)),
            dma((2, steps, CHUNKS, 2)),
            dma((RING - 1,)),
            dma((RING - 1,)),
            dma((CHUNKS, XY_COPIES)),
            dma((CHUNKS, XY_COPIES)),
            dma((2 * PIECES + CHUNKS,)),
            dma((2 * PIECES + CHUNKS,)),
            dma((2 * PIECES,)),
            dma((CHUNKS,)),
            dma((2, steps, CHUNKS, 2)),
            dma((2, steps, CHUNKS, 2)),
            dma((CHUNKS, XY_COPIES)),
            dma((CHUNKS, XY_COPIES)),
        ],
        compiler_params=pltpu.CompilerParams(
            collective_id=0, has_side_effects=True, vmem_limit_bytes=60 << 20
        ),
        name="layer",
    )(tokens, ids, gates, expert, w_in, w_out)


def local(tokens, gates, expert_ids, slot_expert, w_in, w_out):
    expert = slot_expert.reshape(1, -1)
    return layer(tokens, expert_ids.T, gates.T, expert, w_in, w_out)


def solution(mesh):
    return jax.shard_map(
        local,
        mesh=mesh,
        in_specs=(
            P(("dp", "ep"), None),
            P(("dp", "ep"), None),
            P(("dp", "ep"), None),
            P("dp"),
            P(("dp", "ep"), None, None, None),
            P(("dp", "ep"), None, None),
        ),
        out_specs=P(("dp", "ep"), None),
        check_vma=False,
    )
```

```python
import jax
import jax.numpy as jnp
from jax import lax
from jax.experimental import pallas as pl
from jax.experimental.pallas import tpu as pltpu
from jax.sharding import PartitionSpec as P

MESH = pl.DeviceIdType.MESH
GROUP = 4
CAPE = 20
Z = 16
X = 4
Y = 2
RING = Z // 2
COLS = X * Y
WIDTHS = (512, 512, 512, 512)
CHUNKS = len(WIDTHS)
PIECES = 4
SKEW = 1
EARLY = (0, 2, 2, 2)


def z_place():
    me = lax.axis_index("ep")
    z = me % Z
    return me - z, z


def neighbours():
    base, z = z_place()
    return base + (z + 2) % Z, base + (z + Z - 2) % Z


def signal_all(devices):
    barrier = pltpu.get_barrier_semaphore()
    for device in devices:
        pl.semaphore_signal(barrier, inc=1, device_id={"ep": device}, device_id_type=MESH)
    pl.semaphore_wait(barrier, len(devices))


def columns():
    me = lax.axis_index("ep")
    return me // (X * Z), me // Z % X, me % Z


def column_at(y, x):
    return y % Y * X + x % X


def xy_peers():
    y, x, z = columns()
    return [
        column_at(y + ky, x + kx) * Z + z for ky in range(Y) for kx in range(X) if kx or ky
    ]


def xy_copies(send_ref, recv_ref, relay_ref, send_sem, recv_sem):
    y, x, z = columns()
    mine = column_at(y, x)
    half = send_ref.shape[1] // 2

    def remote(k, src, dst, column):
        return pltpu.make_async_remote_copy(
            src_ref=src,
            dst_ref=dst,
            send_sem=send_sem.at[k],
            recv_sem=recv_sem.at[k],
            device_id={"ep": column * Z + z},
            device_id_type=MESH,
        )

    relays, forwards, direct = [], [], []
    for way, step in ((0, 1), (1, X - 1)):
        rows = pl.ds(way * half, half)
        for ky in range(Y):
            k = 2 * way + ky
            slot = relay_ref.at[k]
            relays.append(
                remote(k, send_ref.at[column_at(y + ky, x + 2), rows], slot, column_at(y, x + step))
            )
            forwards.append(
                remote(
                    4 + k,
                    slot,
                    recv_ref.at[column_at(y, x + X - step), rows],
                    column_at(y + ky, x + step),
                )
            )
    for k, (ky, kx) in enumerate(((1, 1), (1, 3), (1, 0), (0, 1), (0, 3))):
        other = column_at(y + ky, x + kx)
        direct.append(remote(8 + k, send_ref.at[other], recv_ref.at[mine], other))
    return relays, forwards, direct


XY_COPIES = 13


def layer_kernel(
    tok_ref, ids_hbm, gates_hbm, expert_ref, win_ref, wout_ref, out_ref,
    held, ids_ref, gates_ref, table, meta, pick, send, recv, relay, win2, wout2, act, hidden,
    back, relay2, mix, part, come, go,
    own_sem, small_sem, zs_sem, zr_sem, ms_sem, mr_sem, xs_sem, xr_sem, ws_sem, wr_sem, wl_sem, wo_sem,
    rs_sem, rr_sem, bs_sem, br_sem,
):
    base, z = z_place()
    m, member = z // 2, z % 2
    ends = neighbours()
    rows, width = tok_ref.shape
    slots = pick.shape[1]
    half = rows // 2
    last = RING // 2 - 1
    y, x, _ = columns()
    mine = column_at(y, x)
    partner = mine * Z + z + 1 - 2 * member

    def span(chunk):
        return pl.ds(sum(WIDTHS[:chunk]), WIDTHS[chunk])

    own = []
    for chunk in range(CHUNKS):
        own.append(
            pltpu.make_async_copy(
                tok_ref.at[:, span(chunk)], held[chunk].at[pl.ds(m * rows, rows)], own_sem.at[chunk]
            )
        )
        own[-1].start()
    small = [
        pltpu.make_async_copy(ids_hbm, ids_ref, small_sem.at[0]),
        pltpu.make_async_copy(gates_hbm, gates_ref, small_sem.at[1]),
    ]
    for piece in small:
        piece.start()
    ff = win_ref.shape[2]
    mine_out = pl.ds(member * ff, ff)
    own_out = []
    for chunk in range(CHUNKS):
        own_out.append(
            pltpu.make_async_copy(
                wout_ref.at[0, :, span(chunk)], wout2[chunk].at[mine_out], wo_sem.at[chunk]
            )
        )
        own_out[-1].start()
    ring = [base + (z + 2 * k) % Z for k in range(1, RING)]
    signal_all(ring + [partner] + xy_peers())

    z_sent, started = {}, []

    def z_go(chunk, step):
        if step == 0:
            own[chunk].wait()
        for part_of in (0, 1):
            for way in (0, 1):
                if step == last and way != part_of:
                    continue
                if step:
                    z_sent[way, step - 1, chunk, part_of].wait_recv()
                owner = (m + (RING - step if way == 0 else step)) % RING
                there = held[chunk].at[pl.ds(owner * rows + part_of * half, half)]
                sent = pltpu.make_async_remote_copy(
                    src_ref=there,
                    dst_ref=there,
                    send_sem=zs_sem.at[way, step, chunk, part_of],
                    recv_sem=zr_sem.at[way, step, chunk, part_of],
                    device_id={"ep": ends[way]},
                    device_id_type=MESH,
                )
                sent.start()
                z_sent[way, step, chunk, part_of] = sent
                started.append(sent)

    queue = sorted(
        ((chunk, step) for chunk in range(CHUNKS) for step in range(last + 1)),
        key=lambda place: (SKEW * place[0] + place[1], place[0]),
    )
    z_go(*queue.pop(0))

    for piece in small:
        piece.wait()
    groups = Z // GROUP * COLS
    line = lax.broadcasted_iota(jnp.int32, (groups, groups), 0)
    wanted = lax.broadcasted_iota(jnp.int32, (groups, groups), 1) == (
        line % COLS * (Z // GROUP) + line // COLS
    )
    expert = jnp.sum(
        jnp.where(wanted, expert_ref[...].astype(jnp.float32), 0.0), axis=1, keepdims=True
    ).astype(jnp.int32)
    chosen = jnp.zeros((groups, rows), jnp.float32)
    gate = jnp.zeros((groups, rows), jnp.float32)
    for k in range(ids_ref.shape[0]):
        same = ids_ref[pl.ds(k, 1), :] == expert
        chosen += jnp.where(same, 1.0, 0.0)
        gate += jnp.where(same, gates_ref[pl.ds(k, 1), :], 0.0)
    earlier = lax.broadcasted_iota(jnp.int32, (rows, rows), 0) < lax.broadcasted_iota(
        jnp.int32, (rows, rows), 1
    )
    rank = jnp.dot(
        chosen.astype(jnp.bfloat16),
        jnp.where(earlier, 1.0, 0.0).astype(jnp.bfloat16),
        preferred_element_type=jnp.float32,
    )
    slot = jnp.where(chosen > 0.5, rank + (m * CAPE).astype(jnp.float32), -1.0)
    table[:, 0] = jnp.concatenate([slot, slot], axis=1).reshape(Z // GROUP, COLS, 2 * rows)
    table[:, 1] = jnp.concatenate([gate, gate], axis=1).reshape(Z // GROUP, COLS, 2 * rows)
    metas = []
    for k in range(1, RING):
        other = (m + k) % RING
        metas.append(
            pltpu.make_async_remote_copy(
                src_ref=table.at[other // 2],
                dst_ref=meta.at[m],
                send_sem=ms_sem.at[k - 1],
                recv_sem=mr_sem.at[k - 1],
                device_id={"ep": base + (z + 2 * k) % Z},
                device_id_type=MESH,
            )
        )
        metas[-1].start()
    meta[m] = table[m // 2]

    def paired(pair, kind):
        left = lax.broadcasted_iota(jnp.int32, (COLS, 2 * rows), 1) < rows
        return jnp.where(left, meta[2 * pair, kind], meta[2 * pair + 1, kind])

    def build_pick():
        for pair in range(RING // 2):
            both = paired(pair, 0)
            place = lax.broadcasted_iota(jnp.int32, (slots, 2 * rows), 0).astype(jnp.float32)
            for column in range(COLS):
                hit = place == jnp.broadcast_to(both[column : column + 1], place.shape)
                pick[column, :, pl.ds(pair * 2 * rows, 2 * rows)] = jnp.where(
                    hit, 1.0, 0.0
                ).astype(jnp.bfloat16)

    def build_mix():
        for pair in range(RING // 2):
            slot, gate = paired(pair, 0), paired(pair, 1)
            first = lax.broadcasted_iota(jnp.int32, slot.shape, 0) * slots
            slot = jnp.where(slot < 0.0, -1.0, slot + first.astype(jnp.float32)).T
            gate = gate.T
            high = gate.astype(jnp.bfloat16).astype(jnp.float32)
            low = gate - high
            for lane in range(0, COLS * slots, 128):
                place = lax.broadcasted_iota(jnp.int32, (2 * rows, 128), 1) + lane
                place = place.astype(jnp.float32)
                tops = jnp.zeros(place.shape, jnp.float32)
                rest = jnp.zeros(place.shape, jnp.float32)
                for column in range(lane // slots, (lane + 127) // slots + 1):
                    hit = place == slot[:, column : column + 1]
                    tops += jnp.where(hit, high[:, column : column + 1], 0.0)
                    rest += jnp.where(hit, low[:, column : column + 1], 0.0)
                here = pl.ds(pair * 2 * rows, 2 * rows), pl.ds(lane, 128)
                mix[0, here[0], here[1]] = tops.astype(jnp.bfloat16)
                mix[1, here[0], here[1]] = rest.astype(jnp.bfloat16)

    count = ff // PIECES
    pieces = []
    for piece in range(PIECES):
        here = pl.ds(piece * count, count)
        for side in (0, 1):
            there = pl.ds((2 * side + member) * ff + piece * count, count)
            pieces.append((win_ref.at[0, side, here], win2.at[there]))
    for chunk in range(CHUNKS):
        there = wout2[chunk].at[mine_out]
        pieces.append((there, there))
    weights, kept = [], []

    def weight_go(src, dst):
        k = len(weights)
        weights.append(
            pltpu.make_async_remote_copy(
                src_ref=src,
                dst_ref=dst,
                send_sem=ws_sem.at[k],
                recv_sem=wr_sem.at[k],
                device_id={"ep": partner},
                device_id_type=MESH,
            )
        )
        if k < 2 * PIECES:
            kept.append(pltpu.make_async_copy(src, dst, wl_sem.at[k]))
            kept[-1].start()
        else:
            own_out[k - 2 * PIECES].wait()
        weights[-1].start()

    def forward(copies):
        relays, forwards, _ = copies
        for came, sent in zip(relays, forwards):
            came.wait_recv()
            sent.start()

    exchanges = []
    for chunk in range(CHUNKS):
        while queue and SKEW * queue[0][0] + queue[0][1] <= SKEW * chunk + last:
            if queue[0] == (0, last):
                for sent in metas:
                    sent.wait_recv()
                build_pick()
            z_go(*queue.pop(0))
        for _ in range(EARLY[chunk] if queue else len(pieces)):
            weight_go(*pieces.pop(0))
        if chunk:
            forward(exchanges[-1])
        for way in (0, 1):
            z_sent[way, last - 1, chunk, 1 - way].wait_recv()
            z_sent[way, last, chunk, way].wait_recv()

        @pl.loop(0, COLS)
        def _(column):
            send[chunk][column] = jnp.dot(
                pick[column], held[chunk][...], preferred_element_type=jnp.float32
            ).astype(jnp.bfloat16)

        copies = xy_copies(
            send[chunk], recv[chunk], relay[chunk], xs_sem.at[chunk], xr_sem.at[chunk]
        )
        for sent in copies[0] + copies[2]:
            sent.start()
        exchanges.append(copies)
        recv[chunk][mine] = send[chunk][mine]
    build_mix()
    forward(exchanges[-1])

    tile = COLS * slots // 4
    group = COLS // 4
    for k in range(2 * PIECES):
        weights[k].wait_recv()
        kept[k].wait()
    for chunk in range(CHUNKS):
        _, forwards, direct = exchanges[chunk]
        for sent in direct + forwards:
            sent.wait_recv()

        @pl.loop(0, 4)
        def _(step):
            here = pl.ds(pl.multiple_of(step * tile, tile), tile)
            term = lax.dot_general(
                recv[chunk][pl.ds(step * group, group)].reshape(tile, WIDTHS[chunk]),
                win2[:, span(chunk)],
                (((1,), (1,)), ((), ())),
                preferred_element_type=jnp.float32,
            )
            if chunk:
                term += act[here]
            if chunk < CHUNKS - 1:
                act[here] = term
            else:
                side = hidden.shape[1]
                value = term[:, :side]
                value = value / (1.0 + jnp.exp(-value)) * term[:, side:]
                hidden[here] = value.astype(jnp.bfloat16)

    for relays, forwards, direct in exchanges:
        for sent in relays + forwards + direct:
            sent.wait_send()

    exchanges, r_sent = [], {}

    def produce(chunk):
        weights[2 * PIECES + chunk].wait_recv()

        @pl.loop(0, 4)
        def _(step):
            here = pl.ds(pl.multiple_of(step * tile, tile), tile)
            send[chunk][pl.ds(step * group, group)] = (
                jnp.dot(hidden[here], wout2[chunk][...], preferred_element_type=jnp.float32)
                .astype(jnp.bfloat16)
                .reshape(group, slots, WIDTHS[chunk])
            )

        copies = xy_copies(
            send[chunk], back[chunk], relay2[chunk], bs_sem.at[chunk], br_sem.at[chunk]
        )
        for sent in copies[0] + copies[2]:
            sent.start()
        exchanges.append(copies)
        back[chunk][mine] = send[chunk][mine]

    def merge(chunk):
        _, forwards, direct = exchanges[chunk]
        for sent in direct + forwards:
            sent.wait_recv()
        block = 256

        @pl.loop(0, RING * rows // block)
        def _(step):
            here = pl.ds(pl.multiple_of(step * block, block), block)
            values = back[chunk][...].reshape(COLS * slots, WIDTHS[chunk])
            part[chunk][here] = jnp.dot(
                mix[0, here], values, preferred_element_type=jnp.float32
            ) + jnp.dot(mix[1, here], values, preferred_element_type=jnp.float32)

    def reduce_step(chunk, step):
        for part_of in (0, 1):
            local = pl.ds(part_of * half, half)
            for way in (0, 1):
                if step == 0 and way != part_of:
                    continue
                ahead = RING // 2 - step
                target = (m + (ahead if way == 0 else RING - ahead)) % RING
                value = part[chunk][pl.ds(target * rows + part_of * half, half)]
                before = r_sent.get((way, step - 1, chunk, part_of))
                if before is not None:
                    before.wait_recv()
                    value += come[chunk][way, step - 1, local].astype(jnp.float32)
                go[chunk][way, step, local] = value.astype(jnp.bfloat16)
                sent = pltpu.make_async_remote_copy(
                    src_ref=go[chunk].at[way, step, local],
                    dst_ref=come[chunk].at[way, step, local],
                    send_sem=rs_sem.at[way, step, chunk, part_of],
                    recv_sem=rr_sem.at[way, step, chunk, part_of],
                    device_id={"ep": ends[way]},
                    device_id_type=MESH,
                )
                sent.start()
                started.append(sent)
                r_sent[way, step, chunk, part_of] = sent

    def finish(chunk):
        total = part[chunk][pl.ds(m * rows, rows)]
        for way in (0, 1):
            for part_of in (0, 1):
                r_sent[way, last, chunk, part_of].wait_recv()
            total += come[chunk][way, last].astype(jnp.float32)
        out_ref[:, span(chunk)] = total.astype(jnp.bfloat16)

    produce(0)
    forward(exchanges[0])
    produce(1)
    for chunk in range(CHUNKS):
        merge(chunk)
        reduce_step(chunk, 0)
        if chunk:
            reduce_step(chunk - 1, 2)
        if chunk + 1 < CHUNKS:
            forward(exchanges[chunk + 1])
        if chunk + 2 < CHUNKS:
            produce(chunk + 2)
        reduce_step(chunk, 1)
        if chunk:
            reduce_step(chunk - 1, 3)
        if chunk > 1:
            finish(chunk - 2)
    reduce_step(CHUNKS - 1, 2)
    finish(CHUNKS - 2)
    reduce_step(CHUNKS - 1, 3)
    finish(CHUNKS - 1)
    for relays, forwards, direct in exchanges:
        for sent in relays + forwards + direct:
            sent.wait_send()
    for sent in started + metas + weights:
        sent.wait_send()


def layer(tokens, ids, gates, expert, w_in, w_out):
    rows, width = tokens.shape
    _, two, ff, _ = w_in.shape
    slots = RING * CAPE
    steps = RING // 2
    kind = tokens.dtype
    dma = pltpu.SemaphoreType.DMA

    def per_chunk(*lead, kind=kind):
        return [pltpu.VMEM(lead + (size,), kind) for size in WIDTHS]

    return pl.pallas_call(
        layer_kernel,
        out_shape=jax.ShapeDtypeStruct((rows, width), kind),
        in_specs=[pl.BlockSpec(memory_space=pl.ANY)] * 3
        + [pl.BlockSpec(memory_space=pltpu.VMEM)]
        + [pl.BlockSpec(memory_space=pl.ANY)] * 2,
        out_specs=pl.BlockSpec(memory_space=pltpu.VMEM),
        scratch_shapes=[
            per_chunk(RING * rows),
            pltpu.VMEM(ids.shape, ids.dtype),
            pltpu.VMEM(gates.shape, gates.dtype),
            pltpu.VMEM((Z // GROUP, 2, COLS, 2 * rows), jnp.float32),
            pltpu.VMEM((RING, 2, COLS, 2 * rows), jnp.float32),
            pltpu.VMEM((COLS, slots, RING * rows), kind),
            per_chunk(COLS, slots),
            per_chunk(COLS, slots),
            per_chunk(2 * Y, slots // 2),
            pltpu.VMEM((two * 2 * ff, width), kind),
            per_chunk(2 * ff),
            pltpu.VMEM((COLS * slots, two * 2 * ff), jnp.float32),
            pltpu.VMEM((COLS * slots, 2 * ff), kind),
            per_chunk(COLS, slots),
            per_chunk(2 * Y, slots // 2),
            pltpu.VMEM((2, RING * rows, COLS * slots), kind),
            per_chunk(RING * rows, kind=jnp.float32),
            per_chunk(2, steps, rows),
            per_chunk(2, steps, rows),
            dma((CHUNKS,)),
            dma((2,)),
            dma((2, steps, CHUNKS, 2)),
            dma((2, steps, CHUNKS, 2)),
            dma((RING - 1,)),
            dma((RING - 1,)),
            dma((CHUNKS, XY_COPIES)),
            dma((CHUNKS, XY_COPIES)),
            dma((2 * PIECES + CHUNKS,)),
            dma((2 * PIECES + CHUNKS,)),
            dma((2 * PIECES,)),
            dma((CHUNKS,)),
            dma((2, steps, CHUNKS, 2)),
            dma((2, steps, CHUNKS, 2)),
            dma((CHUNKS, XY_COPIES)),
            dma((CHUNKS, XY_COPIES)),
        ],
        compiler_params=pltpu.CompilerParams(
            collective_id=0, has_side_effects=True, vmem_limit_bytes=60 << 20
        ),
        name="layer",
    )(tokens, ids, gates, expert, w_in, w_out)


def local(tokens, gates, expert_ids, slot_expert, w_in, w_out):
    expert = slot_expert.reshape(1, -1)
    return layer(tokens, expert_ids.T, gates.T, expert, w_in, w_out)


def solution(mesh):
    return jax.shard_map(
        local,
        mesh=mesh,
        in_specs=(
            P(("dp", "ep"), None),
            P(("dp", "ep"), None),
            P(("dp", "ep"), None),
            P("dp"),
            P(("dp", "ep"), None, None, None),
            P(("dp", "ep"), None, None),
        ),
        out_specs=P(("dp", "ep"), None),
        check_vma=False,
    )
```
